128 devices in a mesh: shard: 8 (over y_lo, z), ctx: 8 (over y_hi, x), tp: 2 (over core).
Axes of the slice: x: 4, y: 4 (y_hi: 2, y_lo: 2; y = y_hi * 2 + y_lo), z: 4, core: 2. Of those that a mesh axis runs over, the one named last changes fastest.
Arguments:
- tokens: bfloat16 [8, 2048, 2048], P('shard', 'ctx'), may hold values from -6 to 6
- cotangent: bfloat16 [8, 2048, 2048], P('shard', 'ctx'), may hold values from -6 to 6
- seq_ids: int32 [8, 2048], P('shard'), may hold values from 0 to 1, as said below
- block_ids: int32 [8, 2048], P('shard'), may hold values from 0 to 7, as said below
- keep_layer: int32 [8], P('shard'), may hold values from 0 to 1, as said below
- gain_attn: float32 [2048], replicated, may hold values from 0.25 to 1.75
- gain_ffn: float32 [2048], replicated, may hold values from 0.25 to 1.75
- w_query: float32 [2048, 2048], P('shard', 'tp'), may hold values from -0.125 to 0.125
- w_key: float32 [2048, 512], P('shard', 'tp'), may hold values from -0.125 to 0.125
- w_value: float32 [2048, 512], P('shard', 'tp'), may hold values from -0.125 to 0.125
- w_out: float32 [2048, 2048], P('shard', 'tp'), may hold values from -0.75 to 0.75
- w_gate: float32 [2048, 5632], P('shard', 'tp'), may hold values from -0.125 to 0.125
- w_up: float32 [2048, 5632], P('shard', 'tp'), may hold values from -0.125 to 0.125
- w_down: float32 [2048, 5632], P('shard', 'tp'), may hold values from -0.078125 to 0.078125
Outputs:
- output: bfloat16 [8, 2048, 2048], P('shard', 'ctx')
- input_grad: bfloat16 [8, 2048, 2048], P('shard', 'ctx')
- grad_gain_attn: float32 [2048], P('shard')
- grad_gain_ffn: float32 [2048], P('shard')
- grad_query: float32 [2048, 2048], P('shard', 'tp')
- grad_key: float32 [2048, 512], P('shard', 'tp')
- grad_value: float32 [2048, 512], P('shard', 'tp')
- grad_out: float32 [2048, 2048], P('shard', 'tp')
- grad_gate: float32 [2048, 5632], P('shard', 'tp')
- grad_up: float32 [2048, 5632], P('shard', 'tp')
- grad_down: float32 [2048, 5632], P('shard', 'tp')
The draws below stay inside these ranges and needn't reach their ends.
Inputs may be any that keep to these rules, and one draw needn't show every extreme that they name: `seq_ids`: each sample holds exactly two documents: id 0 on a leading run of fewer than min(256, 256) positions, id 1 on the rest. Blocks of 256 positions are counted from each document's start: block_ids[p] = (p - start of p's document) // 256. `keep_layer`: at least one sample runs the layer and at least one skips it.
All inputs are finite; a program needn't handle non-finite values.
Results may differ from the reference program's by a relative error of at most 0.02.
Values may be sent and summed in bfloat16 or wider, within the bound.
No kernel may reach another device: no remote copies, remote signals or barrier semaphores. Data moves between devices by JAX's collectives and lax.ppermute only.
A program may use at most 256 MiB of HBM per device.

```python
import jax
import jax.numpy as jnp
from jax import lax

D = 2048
H = 16
KVH = 4
HD = 128
FF = 5632
BLK = 256
TOK_DEV = 256
LEN = 2048
SAMPLES = 8


def doc_layout(key):
    cut = jax.random.randint(jax.random.fold_in(key, 11), (SAMPLES, 1), 1, min(TOK_DEV, BLK))
    position = jnp.arange(LEN, dtype=jnp.int32)[None, :]
    later = position >= cut
    segment = later.astype(jnp.int32)
    block_index = jnp.where(later, (position - cut) // BLK, position // BLK).astype(jnp.int32)
    return (segment, block_index)


def draw_seq_ids(key, part):
    return doc_layout(key)[0]


def draw_block_ids(key, part):
    return doc_layout(key)[1]


def draw_keep_layer(key, part):
    bits = jax.random.randint(jax.random.fold_in(key, 21), (SAMPLES,), 0, 2).astype(jnp.int32)
    first = jax.random.randint(jax.random.fold_in(key, 22), (), 0, SAMPLES)
    offset = jax.random.randint(jax.random.fold_in(key, 23), (), 0, SAMPLES - 1)
    second = (first + 1 + offset) % SAMPLES
    bits = bits.at[first].set(1)
    bits = bits.at[second].set(0)
    return bits.astype(jnp.int32)


def level_of(rng, dims, pieces, least, top_value):
    level, own = 1.0, jax.random.fold_in(rng, 6)
    for axis_at, shards_of in pieces:
        steps = jnp.exp(jax.random.uniform(jax.random.fold_in(own, axis_at), (shards_of,), jnp.float32, least / len(pieces), top_value / len(pieces)))
        level = level * jnp.repeat(steps, dims[axis_at] // shards_of).reshape([-1 if axis == axis_at else 1 for axis in range(len(dims))])
    return level


def centred(own_key, extent, deviation, most, cuts=(), kind=jnp.bfloat16):
    level = level_of(own_key, extent, cuts, -0.22, 0.18) if cuts else 1.0
    drawn = jax.random.normal(own_key, extent, jnp.float32) * deviation * level
    return jnp.minimum(jnp.maximum(drawn, -most), most).astype(kind)


def setup_inputs(seed: int = 0) -> dict:
    key_of = jax.random.split(jax.random.key(seed), 15)
    return {
        "tokens": centred(key_of[0], (SAMPLES, LEN, D), 1.0, 6.0, ((0, 8), (1, 8))),
        "cotangent": centred(key_of[1], (SAMPLES, LEN, D), 1.0, 6.0, ((0, 8), (1, 8))),
        "seq_ids": draw_seq_ids(jax.random.fold_in(key_of[14], 71), 0),
        "block_ids": draw_block_ids(jax.random.fold_in(key_of[14], 71), 0),
        "keep_layer": draw_keep_layer(jax.random.fold_in(key_of[14], 71), 0),
        "gain_attn": jnp.clip(1.0 + 0.15 * jax.random.normal(key_of[5], (D,), jnp.float32), 0.25, 1.75),
        "gain_ffn": jnp.clip(1.0 + 0.15 * jax.random.normal(key_of[6], (D,), jnp.float32), 0.25, 1.75),
        "w_query": centred(key_of[7], (D, H * HD), D ** -0.5, 0.125, ((0, 8), (1, 2)), jnp.float32),
        "w_key": centred(key_of[8], (D, KVH * HD), D ** -0.5, 0.125, ((0, 8), (1, 2)), jnp.float32),
        "w_value": centred(key_of[9], (D, KVH * HD), D ** -0.5, 0.125, ((0, 8), (1, 2)), jnp.float32),
        "w_out": centred(key_of[10], (D, H * HD), (H * HD // 32) ** -0.5, 0.75, ((0, 8), (1, 2)), jnp.float32),
        "w_gate": centred(key_of[11], (D, FF), D ** -0.5, 0.125, ((0, 8), (1, 2)), jnp.float32),
        "w_up": centred(key_of[12], (D, FF), D ** -0.5, 0.125, ((0, 8), (1, 2)), jnp.float32),
        "w_down": centred(key_of[13], (D, FF), FF ** -0.5, 0.078125, ((0, 8), (1, 2)), jnp.float32),
    }


EPS = 1e-05
NEG = -1e+30

@jax.custom_vjp
def low(v):
    return lax.optimization_barrier(v.astype(jnp.bfloat16)).astype(jnp.float32)

@jax.custom_vjp
def low_back(v):
    return v

def low_keep(v):
    return (low(v), None)

def low_pass(kept, grad):
    return (grad,)

def back_keep(v):
    return (v, None)

def back_low(kept, grad):
    return (low(grad),)
low.defvjp(low_keep, low_pass)
low_back.defvjp(back_keep, back_low)

def matmul(left, right):
    return jnp.dot(left, right, precision=lax.Precision.HIGHEST, preferred_element_type=jnp.float32)

def matmul_tr(left, right):
    return jnp.dot(left, right.T, precision=lax.Precision.HIGHEST, preferred_element_type=jnp.float32)

def rms_norm(value, gain):
    return value * lax.rsqrt(lax.optimization_barrier(jnp.mean(value * value, axis=-1, keepdims=True)) + EPS) * gain

def rope_tables(positions):
    freqs = 10000.0 ** (-(jnp.arange(HD // 2).astype(jnp.float32) * 2.0 / HD))
    angle = positions[:, None] * freqs[None, :]
    cosine = jnp.concatenate([jnp.cos(angle), jnp.cos(angle)], axis=-1)
    sine = jnp.concatenate([jnp.sin(angle), jnp.sin(angle)], axis=-1)
    return (cosine, sine)

def rotate(value, cosine, sine):
    half = value.shape[-1] // 2
    turned = jnp.concatenate([-value[..., half:], value[..., :half]], axis=-1)
    return value * cosine[:, None, :] + turned * sine[:, None, :]

def layer(xval, gain_attn, gain_ffn, w_query, w_key, w_value, w_out, w_gate, w_up, w_down, seg, blk, keep_flag):
    length = xval.shape[0]
    groups = H // KVH
    cosine, sine = rope_tables(jnp.arange(length).astype(jnp.float32))
    normed = low(rms_norm(xval, gain_attn))
    query = low_back(matmul(normed, low(w_query)))
    keys = low_back(matmul(normed, low(w_key)))
    values = low(low_back(matmul(normed, low(w_value))))
    query = low(rotate(query.reshape(length, H, HD), cosine, sine)).reshape(length, KVH, groups, HD)
    keys = low(rotate(keys.reshape(length, KVH, HD), cosine, sine))
    values = values.reshape(length, KVH, HD)
    block_rows = min(512, length)
    nblocks = length // block_rows

    def attend(item):
        q_block, seg_block, blk_block = item
        raw = jnp.einsum('qgrd,kgd->grqk', q_block, keys, precision=lax.Precision.HIGHEST)
        scores = low_back(raw) * HD ** (-0.5)
        allowed = (seg_block[:, None] == seg[None, :]) & (blk[None, :] <= blk_block[:, None])
        safe = jnp.where(allowed, scores, NEG)
        top = lax.optimization_barrier(jnp.max(safe, axis=-1, keepdims=True))
        expo = jnp.where(allowed, jnp.exp(safe - top), 0.0)
        probs = expo / lax.optimization_barrier(jnp.sum(expo, axis=-1, keepdims=True))
        mixed = jnp.einsum('grqk,kgd->qgrd', low(probs), values, precision=lax.Precision.HIGHEST)
        return mixed.reshape(block_rows, H * HD)
    heads = lax.map(jax.checkpoint(attend), (query.reshape(nblocks, block_rows, KVH, groups, HD), seg.reshape(nblocks, block_rows), blk.reshape(nblocks, block_rows)))
    heads = low(low_back(heads.reshape(length, H * HD)))
    attn_branch = low_back(matmul_tr(heads, low(w_out)))
    middle = xval + keep_flag * attn_branch
    normed_ffn = low(rms_norm(middle, gain_ffn))
    gate = low_back(matmul(normed_ffn, low(w_gate)))
    up_val = low_back(matmul(normed_ffn, low(w_up)))
    hidden = low(jax.nn.silu(gate) * up_val)
    ffn_branch = low_back(matmul_tr(hidden, low(w_down)))
    return middle + keep_flag * ffn_branch

def reference(tokens, cotangent, seq_ids, block_ids, keep_layer, gain_attn, gain_ffn, w_query, w_key, w_value, w_out, w_gate, w_up, w_down):
    params = (gain_attn, gain_ffn, w_query, w_key, w_value, w_out, w_gate, w_up, w_down)

    def sample_step(totals, item):
        sample_x, sample_cot, seg, blk, keep_int = item
        keep_flag = keep_int.astype(jnp.float32)

        def forward(xval, *weights):
            return layer(xval, *weights, seg, blk, keep_flag)
        result, pullback = jax.vjp(forward, sample_x.astype(jnp.float32), *params)
        gradients = pullback(sample_cot.astype(jnp.float32))
        totals = jax.tree.map(lambda left, right: left + right, totals, tuple(gradients[1:]))
        return (totals, (result.astype(jnp.bfloat16), gradients[0].astype(jnp.bfloat16)))
    initial = tuple((jnp.zeros_like(param) for param in params))
    totals, (outputs, input_grads) = lax.scan(sample_step, initial, (tokens, cotangent, seq_ids, block_ids, keep_layer))
    return (outputs, input_grads, totals[0], totals[1], totals[2], totals[3], totals[4], totals[5], totals[6], totals[7], totals[8])
```

```python
import jax
import jax.numpy as jnp
from jax import lax
from jax.sharding import Mesh, PartitionSpec as P

HD = 128
EPS = 1e-05
NEG = -1e30
F32 = jnp.float32
BF16 = jnp.bfloat16
SHARD = ("yl", "z")
SWAP = ((0, 1), (1, 0))


def half(value):
    return value.astype(BF16)


def mm(left, right):
    return jnp.dot(left, right, preferred_element_type=F32)


def mm_nt(left, right):
    return lax.dot_general(left, right, (((1,), (1,)), ((), ())), preferred_element_type=F32)


def mm_tn(left, right):
    return lax.dot_general(left, right, (((0,), (0,)), ((), ())), preferred_element_type=F32)


def swap_cores(value):
    return lax.ppermute(value, "tp", SWAP)


def shift_x(value, hop):
    return lax.ppermute(value, "x", [(i, (i + hop) % 4) for i in range(4)])


def gather_x(value):
    return [value] + [shift_x(value, -hop) for hop in (1, 2, 3)]


def scatter_x(chunks):
    moved = [shift_x(half(chunks[hop]), hop) for hop in (2, 1, 3)]
    return chunks[0] + moved[0].astype(F32) + moved[1].astype(F32) + moved[2].astype(F32)


def absolute(chunks, x_at):
    stacked = jnp.stack(chunks + chunks[:3])
    return lax.dynamic_slice_in_dim(stacked, (4 - x_at) % 4, 4, axis=0)


def rotate(value, cosine, sine):
    turned = jnp.concatenate([-value[..., HD // 2 :], value[..., : HD // 2]], axis=-1)
    return value * cosine + turned * sine


def unrotate(grad, cosine, sine):
    scaled = grad * sine
    return grad * cosine + jnp.concatenate(
        [scaled[..., HD // 2 :], -scaled[..., : HD // 2]], axis=-1
    )


def norm_root(value):
    return lax.rsqrt(jnp.mean(value * value, axis=-1, keepdims=True) + EPS)


def norm_backward(value, root, gain, grad):
    scaled = gain * grad
    grad_value = root * scaled - value * root**3 * jnp.mean(
        scaled * value, axis=-1, keepdims=True
    )
    return grad_value, jnp.sum(grad * value * root, axis=0)


def per_device(
    tokens, cotangent, seq_ids, block_ids, keep_layer, gain_attn, gain_ffn,
    w_query, w_key, w_value, w_out, w_gate, w_up, w_down,
):
    core, x_at, y_at = lax.axis_index("tp"), lax.axis_index("x"), lax.axis_index("yh")
    first = core == 0
    rows = tokens.shape[1] // 2
    width = tokens.shape[2]
    keep = keep_layer[0].astype(F32)
    scale = HD ** (-0.5)

    side = x_at // 2
    at = x_at % 2
    wq = half(lax.dynamic_slice_in_dim(w_query, at * 512, 512, axis=1))
    wk = half(lax.dynamic_slice_in_dim(w_key, at * HD, HD, axis=1))
    wv = half(lax.dynamic_slice_in_dim(w_value, at * HD, HD, axis=1))
    wo = half(lax.dynamic_slice_in_dim(w_out, at * 512, 512, axis=1))
    pack0 = jnp.concatenate([wq[:, :256], wk, wo[:, :256]], axis=1)
    pack1 = jnp.concatenate([wq[:, 256:], wv, wo[:, 256:]], axis=1)
    lent = lax.ppermute(
        jnp.where(first, pack1, pack0),
        ("x", "tp"),
        [(2 * i + i // 2, 2 * i + 1 - i // 2) for i in range(4)],
    )
    pack = jnp.where(core == side, jnp.where(first, pack0, pack1), lent)
    pack = lax.all_gather(pack, SHARD, axis=0, tiled=True)
    pack_other = swap_cores(pack)
    att0 = jnp.where(first, pack, pack_other)
    att1 = jnp.where(first, pack_other, pack)
    full_qkv = jnp.concatenate([att0[:, :384], att1[:, :384]], axis=1)
    full_out = jnp.concatenate([att0[:, 384:], att1[:, 384:]], axis=1)

    units = w_gate.shape[1] // 4

    def hidden_units(weight):
        own = half(lax.dynamic_slice_in_dim(weight, x_at * units, units, axis=1))
        own = lax.all_gather(own, SHARD, axis=0, tiled=True)
        return own, swap_cores(own)

    xval = lax.dynamic_slice_in_dim(tokens[0], core * rows, rows, axis=0).astype(F32)
    grad_top = lax.dynamic_slice_in_dim(cotangent[0], core * rows, rows, axis=0).astype(F32)
    root_attn = norm_root(xval)
    normed_attn = jnp.concatenate(gather_x(half(xval * root_attn * gain_attn)), axis=0)
    count = normed_attn.shape[0]

    def of_positions(line, y_index, core_index):
        grid = line.reshape(2, 4, 2, rows)
        picked = lax.dynamic_index_in_dim(grid, y_index, 0, keepdims=False)
        picked = lax.dynamic_index_in_dim(picked, core_index, 1, keepdims=False)
        double = jnp.concatenate([picked, picked], axis=0)
        return lax.dynamic_slice_in_dim(double, x_at, 4, axis=0).reshape(-1)

    corners = ((y_at, core), (y_at, 1 - core), (1 - y_at, core), (1 - y_at, 1 - core))
    seg_query = of_positions(seq_ids[0], y_at, core)
    blk_query = of_positions(block_ids[0], y_at, core)
    seg_keys = jnp.concatenate([of_positions(seq_ids[0], *corner) for corner in corners])
    blk_keys = jnp.concatenate([of_positions(block_ids[0], *corner) for corner in corners])
    allowed = (seg_query[:, None] == seg_keys[None, :]) & (blk_keys[None, :] <= blk_query[:, None])
    position = of_positions(jnp.arange(seq_ids.shape[1], dtype=jnp.int32), y_at, core)
    freqs = 10000.0 ** (-(jnp.arange(HD // 2).astype(F32) * 2.0 / HD))
    angle = position.astype(F32)[:, None] * freqs[None, :]
    cosine = jnp.concatenate([jnp.cos(angle), jnp.cos(angle)], axis=-1)
    sine = jnp.concatenate([jnp.sin(angle), jnp.sin(angle)], axis=-1)

    qkv = mm(normed_attn, full_qkv)
    starts = (0, 128, 384, 512)
    query = jnp.stack([half(rotate(qkv[:, s : s + HD], cosine, sine)) for s in starts])
    keys_values = jnp.concatenate(
        [half(rotate(qkv[:, 256:384], cosine, sine)), half(qkv[:, 640:])], axis=1
    )

    def across_y(value):
        return lax.ppermute(value, "yh", SWAP)

    two_kv = jnp.concatenate([keys_values, across_y(keys_values)], axis=0)
    other_kv = swap_cores(two_kv)
    all_kv = jnp.concatenate(
        [two_kv[:count], other_kv[:count], two_kv[count:], other_kv[count:]], axis=0
    )
    all_keys, all_values = all_kv[:, :HD], all_kv[:, HD:]

    raw = jnp.einsum("htd,nd->htn", query, all_keys, preferred_element_type=F32) * scale
    safe = jnp.where(allowed[None], raw, NEG)
    top = jnp.max(safe, axis=-1, keepdims=True)
    weights = jnp.where(allowed[None], jnp.exp(safe - top), 0.0)
    total = jnp.sum(weights, axis=-1, keepdims=True)
    added = jnp.einsum("htn,nd->htd", half(weights), all_values, preferred_element_type=F32)
    heads_f = added / total
    log_total = top + jnp.log(total)
    heads = half(heads_f.transpose(1, 0, 2).reshape(count, 4 * HD))

    def chunked(value):
        return [value[j * rows : (j + 1) * rows] for j in range(4)]

    attn_branch = scatter_x(chunked(mm_nt(heads, full_out)))
    middle = xval + keep * attn_branch
    root_ffn = norm_root(middle)
    normed_ffn = jnp.concatenate(gather_x(half(middle * root_ffn * gain_ffn)), axis=0)

    full_gate, full_up, full_down = hidden_units(w_gate), hidden_units(w_up), hidden_units(w_down)
    d_ffn = jnp.concatenate(gather_x(half(keep * grad_top)), axis=0)
    branch = 0.0
    d_normed = 0.0
    grads_gate, grads_up, grads_down = [], [], []
    for wg, wu, wd in zip(full_gate, full_up, full_down, strict=True):
        gate = mm(normed_ffn, wg)
        up = mm(normed_ffn, wu)
        sig = jax.nn.sigmoid(gate)
        silu = gate * sig
        hidden = half(silu * up)
        branch = branch + mm_nt(hidden, wd)
        d_hidden = mm(d_ffn, wd)
        d_gate = half(d_hidden * up * sig * (1.0 + gate * (1.0 - sig)))
        d_up = half(d_hidden * silu)
        d_normed = d_normed + mm_nt(d_gate, wg) + mm_nt(d_up, wu)
        grads_gate.append(mm_tn(normed_ffn, d_gate))
        grads_up.append(mm_tn(normed_ffn, d_up))
        grads_down.append(mm_tn(d_ffn, hidden))
    d_normed_ffn = scatter_x(chunked(d_normed))
    ffn_branch = scatter_x(chunked(branch))

    def both_cores(value):
        other = swap_cores(value)
        return jnp.concatenate(
            [jnp.where(first, value, other), jnp.where(first, other, value)], axis=0
        )

    output = both_cores(half(middle + keep * ffn_branch))

    def reduce_columns(mine, theirs):
        value = half(mine + swap_cores(half(theirs)).astype(F32))
        value = lax.psum_scatter(value, SHARD, scatter_dimension=0, tiled=True)
        value = half(value.astype(F32) + across_y(value).astype(F32))
        return absolute(gather_x(value), x_at)

    def units_of(value):
        return jnp.concatenate([value[i] for i in range(4)], axis=1).astype(F32)

    grad_down = units_of(reduce_columns(*grads_down))
    grad_gate = units_of(reduce_columns(*grads_gate))
    grad_up = units_of(reduce_columns(*grads_up))

    mid_part, gain_ffn_local = norm_backward(middle, root_ffn, gain_ffn, d_normed_ffn)
    d_middle = grad_top + mid_part
    d_attn = jnp.concatenate(gather_x(half(keep * d_middle)), axis=0)

    d_heads = half(mm(d_attn, full_out))
    d_heads_g = d_heads.reshape(count, 4, HD).transpose(1, 0, 2)
    row_delta = jnp.sum(d_heads_g.astype(F32) * heads_f, axis=-1, keepdims=True)
    raw = jnp.einsum("htd,nd->htn", query, all_keys, preferred_element_type=F32) * scale
    probs = jnp.where(allowed[None], jnp.exp(raw - log_total), 0.0)
    d_probs = jnp.einsum("htd,nd->htn", d_heads_g, all_values, preferred_element_type=F32)
    d_scores = half(scale * probs * (d_probs - row_delta))
    grad_q = jnp.einsum("htn,nd->htd", d_scores, all_keys, preferred_element_type=F32)
    key_part = jnp.einsum("htn,htd->nd", d_scores, query, preferred_element_type=F32)
    value_part = jnp.einsum("htn,htd->nd", half(probs), d_heads_g, preferred_element_type=F32)
    kv_part = jnp.concatenate([key_part, value_part], axis=1)
    kv_mine = jnp.concatenate([kv_part[:count], kv_part[2 * count : 3 * count]], axis=0)
    kv_theirs = jnp.concatenate([kv_part[count : 2 * count], kv_part[3 * count :]], axis=0)
    kv_two = kv_mine + swap_cores(half(kv_theirs)).astype(F32)
    grad_kv = kv_two[:count] + across_y(half(kv_two[count:])).astype(F32)
    d_q = [half(unrotate(grad_q[h], cosine, sine)) for h in range(4)]
    d_key = half(unrotate(grad_kv[:, :HD], cosine, sine))
    d_qkv = jnp.concatenate([d_q[0], d_q[1], d_key, d_q[2], d_q[3], half(grad_kv[:, HD:])], axis=1)
    d_normed_attn = scatter_x(chunked(mm_nt(d_qkv, full_qkv)))
    grad_qkv = mm_tn(normed_attn, d_qkv)
    grad_o = mm_tn(d_attn, heads)
    grads0 = jnp.concatenate([grad_qkv[:, :384], grad_o[:, :256]], axis=1)
    grads1 = jnp.concatenate([grad_qkv[:, 384:], grad_o[:, 256:]], axis=1)
    packs = reduce_columns(jnp.where(first, grads0, grads1), jnp.where(first, grads1, grads0))
    mine = lax.dynamic_slice_in_dim(packs, 2 * core, 2, axis=0)
    theirs = swap_cores(lax.dynamic_slice_in_dim(packs, 2 - 2 * core, 2, axis=0))
    out0 = jnp.where(first, mine, theirs).astype(F32)
    out1 = jnp.where(first, theirs, mine).astype(F32)
    grad_query = jnp.concatenate(
        [out0[0, :, :256], out1[0, :, :256], out0[1, :, :256], out1[1, :, :256]], axis=1
    )
    grad_key = jnp.concatenate([out0[0, :, 256:384], out0[1, :, 256:384]], axis=1)
    grad_value = jnp.concatenate([out1[0, :, 256:384], out1[1, :, 256:384]], axis=1)
    grad_out = jnp.concatenate(
        [out0[0, :, 384:], out1[0, :, 384:], out0[1, :, 384:], out1[1, :, 384:]], axis=1
    )

    input_part, gain_attn_local = norm_backward(xval, root_attn, gain_attn, d_normed_attn)
    input_grad = both_cores(half(d_middle + input_part))
    gains = lax.psum(
        jnp.stack([gain_attn_local, gain_ffn_local]), ("yl", "z", "yh", "x", "tp")
    )
    owned = width // 8
    gains = lax.dynamic_slice_in_dim(
        gains, (lax.axis_index("yl") * 4 + lax.axis_index("z")) * owned, owned, axis=1
    )
    return (
        output[None], input_grad[None], gains[0], gains[1],
        grad_query, grad_key, grad_value, grad_out, grad_gate, grad_up, grad_down,
    )


def solution(mesh):
    fine = Mesh(mesh.devices.reshape(2, 4, 2, 4, 2), ("yl", "z", "yh", "x", "tp"))
    shard, ctx = ("yl", "z"), ("yh", "x")
    acts, weight = P(shard, ctx, None), P(shard, "tp")
    return jax.shard_map(
        per_device,
        mesh=fine,
        in_specs=(acts, acts, P(shard, None), P(shard, None), P(shard), P(), P()) + (weight,) * 7,
        out_specs=(acts, acts, P(shard), P(shard)) + (weight,) * 7,
        check_vma=False,
    )
```

```python
import functools

import jax
import jax.numpy as jnp
from jax import lax
from jax.experimental import pallas as pl
from jax.experimental.pallas import tpu as pltpu
from jax.sharding import Mesh, PartitionSpec as P

HD = 128
EPS = 1e-05
NEG = -1e30
F32 = jnp.float32
BF16 = jnp.bfloat16
SHARD = ("yl", "z")
SCALE = HD ** (-0.5)
LOG2E = 1.4426950408889634
VMEM = 48 * 2**20
SWAP = ((0, 1), (1, 0))


def half(value):
    return value.astype(BF16)


def mm(left, right):
    return jnp.dot(left, right, preferred_element_type=F32)


def mm_nt(left, right):
    return lax.dot_general(left, right, (((1,), (1,)), ((), ())), preferred_element_type=F32)


def mm_tn(left, right):
    return lax.dot_general(left, right, (((0,), (0,)), ((), ())), preferred_element_type=F32)


def swap_cores(value):
    return lax.ppermute(value, "tp", SWAP)


def across_y(value):
    return lax.ppermute(value, "yh", SWAP)


def after(value, *others):
    zero = sum((other[:1, :1] * 0).astype(value.dtype) for other in others)
    tile = value[:16, :HD] + zero
    return lax.dynamic_update_slice(value, tile, (0, 0))


def shift_x(value, hop):
    return lax.ppermute(value, "x", [(i, (i + hop) % 4) for i in range(4)])


def gather_x(value):
    moved = {hop: shift_x(value, -hop) for hop in (2, 1, 3)}
    return [value, moved[1], moved[2], moved[3]]


def scatter_x(chunks):
    moved = [shift_x(half(chunks[hop]), hop) for hop in (2, 1, 3)]
    return chunks[0] + moved[0].astype(F32) + moved[1].astype(F32) + moved[2].astype(F32)


def absolute(chunks, x_at):
    return [lax.select_n((i - x_at) % 4, *chunks) for i in range(4)]


def gather_shard(value):
    spread = jnp.broadcast_to(value[None], (8, *value.shape))
    return lax.all_to_all(spread, SHARD, 0, 0).reshape(-1, value.shape[1])


def rotate(value, cosine, sine):
    turned = jnp.concatenate([-value[..., HD // 2 :], value[..., : HD // 2]], axis=-1)
    return value * cosine + turned * sine


def unrotate(grad, cosine, sine):
    scaled = grad * sine
    return grad * cosine + jnp.concatenate(
        [scaled[..., HD // 2 :], -scaled[..., : HD // 2]], axis=-1
    )


def norm_root(value):
    return lax.rsqrt(jnp.mean(value * value, axis=-1, keepdims=True) + EPS)


def norm_backward(value, root, gain, grad):
    scaled = gain * grad
    return root * scaled - value * root**3 * jnp.mean(scaled * value, axis=-1, keepdims=True)


def attend_kernel(q_ref, kt_ref, v_ref, bias_ref, mixed_ref, heads_ref, lse_ref):
    raw = jnp.dot(q_ref[...], kt_ref[...], preferred_element_type=F32)
    raw = raw * (SCALE * LOG2E) + bias_ref[...]
    top = jnp.max(raw, axis=-1, keepdims=True)
    weights = jnp.exp2(raw - top)
    total = jnp.sum(weights, axis=-1, keepdims=True)
    mixed = jnp.dot(half(weights), v_ref[...], preferred_element_type=F32) / total
    mixed_ref[...] = mixed
    heads_ref[...] = half(mixed)
    lse_ref[0] = top + jnp.log2(total)


def attend(query, keys_t, values, bias, rows=256):
    count, features = query.shape
    n = values.shape[0]
    part = pl.BlockSpec((rows, HD), lambda j, h: (j, h))
    return pl.pallas_call(
        attend_kernel,
        grid=(count // rows, features // HD),
        in_specs=[
            part,
            pl.BlockSpec((HD, n), lambda j, h: (0, 0)),
            pl.BlockSpec((n, HD), lambda j, h: (0, 0)),
            pl.BlockSpec((rows, n), lambda j, h: (j, 0)),
        ],
        out_specs=[part, part, pl.BlockSpec((1, rows, 1), lambda j, h: (h, j, 0))],
        out_shape=[
            jax.ShapeDtypeStruct((count, features), F32),
            jax.ShapeDtypeStruct((count, features), BF16),
            jax.ShapeDtypeStruct((features // HD, count, 1), F32),
        ],
        compiler_params=pltpu.CompilerParams(vmem_limit_bytes=VMEM),
    )(query, keys_t, values, bias)


def attend_back_kernel(
    q_ref, qt_ref, do_ref, dot_ref, lse_ref, delta_ref, k_ref, kt_ref, v_ref, bias_ref,
    dqt_ref, dk_ref, dv_ref, *, piece,
):
    @pl.when(pl.program_id(0) == 0)
    def _():
        dk_ref[...] = jnp.zeros_like(dk_ref)
        dv_ref[...] = jnp.zeros_like(dv_ref)

    q, qt, d_out, d_out_t = q_ref[...], qt_ref[...], do_ref[...], dot_ref[...]
    lse, delta = lse_ref[0], delta_ref[0]
    grad_qt = jnp.zeros(dqt_ref.shape, F32)
    for at in range(0, k_ref.shape[0], piece):
        part = pl.ds(at, piece)
        raw = jnp.dot(k_ref[part, :], qt, preferred_element_type=F32)
        probs = jnp.exp2(raw * (SCALE * LOG2E) + (bias_ref[part, :] - lse))
        d_probs = jnp.dot(v_ref[part, :], d_out_t, preferred_element_type=F32)
        dv_ref[part, :] += jnp.dot(half(probs), d_out, preferred_element_type=F32)
        d_scores = half(probs * (SCALE * (d_probs - delta)))
        dk_ref[part, :] += jnp.dot(d_scores, q, preferred_element_type=F32)
        grad_qt += jnp.dot(kt_ref[:, part], d_scores, preferred_element_type=F32)
    dqt_ref[...] = grad_qt


def attend_back(query, query_t, d_heads, d_heads_t, lse, delta, keys, keys_t, values, bias_t):
    count, features = query.shape
    n = keys.shape[0]
    row = pl.BlockSpec((count, HD), lambda h: (0, h))
    col = pl.BlockSpec((HD, count), lambda h: (h, 0))
    line = pl.BlockSpec((1, 1, count), lambda h: (h, 0, 0))
    whole = pl.BlockSpec((n, HD), lambda h: (0, 0))
    return pl.pallas_call(
        functools.partial(attend_back_kernel, piece=512),
        grid=(features // HD,),
        in_specs=[
            row, col, row, col, line, line, whole,
            pl.BlockSpec((HD, n), lambda h: (0, 0)), whole,
            pl.BlockSpec((n, count), lambda h: (0, 0)),
        ],
        out_specs=[col, whole, whole],
        out_shape=[
            jax.ShapeDtypeStruct((features, count), F32),
            jax.ShapeDtypeStruct((n, HD), F32),
            jax.ShapeDtypeStruct((n, HD), F32),
        ],
        compiler_params=pltpu.CompilerParams(vmem_limit_bytes=VMEM),
    )(query, query_t, d_heads, d_heads_t, lse, delta, keys, keys_t, values, bias_t)


def per_device(
    tokens, cotangent, seq_ids, block_ids, keep_layer, gain_attn, gain_ffn,
    w_query, w_key, w_value, w_out, w_gate, w_up, w_down,
):
    core, x_at, y_at = lax.axis_index("tp"), lax.axis_index("x"), lax.axis_index("yh")
    first = core == 0
    rows = tokens.shape[1] // 2
    width = tokens.shape[2]
    keep = keep_layer[0].astype(F32)

    own_tokens = lax.dynamic_slice_in_dim(tokens[0], core * rows, rows, axis=0)
    x_all = lax.all_gather(own_tokens, "x", axis=0, tiled=True)
    own_top = lax.dynamic_slice_in_dim(cotangent[0], core * rows, rows, axis=0)
    xval, grad_top = own_tokens.astype(F32), own_top.astype(F32)

    side = x_at // 2
    at = x_at % 2
    wq = half(lax.dynamic_slice_in_dim(w_query, at * 512, 512, axis=1))
    wk = half(lax.dynamic_slice_in_dim(w_key, at * HD, HD, axis=1))
    wv = half(lax.dynamic_slice_in_dim(w_value, at * HD, HD, axis=1))
    wo = half(lax.dynamic_slice_in_dim(w_out, at * 512, 512, axis=1))
    pack0 = jnp.concatenate([wq[:, :256], wk, wo[:, :256]], axis=1)
    pack1 = jnp.concatenate([wq[:, 256:], wv, wo[:, 256:]], axis=1)
    lent = lax.ppermute(
        jnp.where(first, pack1, pack0),
        ("x", "tp"),
        [(2 * i + i // 2, 2 * i + 1 - i // 2) for i in range(4)],
    )
    pack = jnp.where(core == side, jnp.where(first, pack0, pack1), lent)
    pack = gather_shard(pack)

    units = w_gate.shape[1] // 4
    tiles = units // HD * HD
    spare = units - tiles
    split = tiles + HD

    def hidden_units(weight):
        main = lax.dynamic_slice_in_dim(weight, x_at * tiles, tiles, axis=1)
        rest = lax.dynamic_slice_in_dim(weight[:, 4 * tiles :], x_at * spare, spare, axis=1)
        return jnp.concatenate([half(main), jnp.pad(half(rest), ((0, 0), (0, HD - spare)))], axis=1)

    own_down = lax.all_gather(after(hidden_units(w_down), x_all), SHARD, axis=0, tiled=True)
    own_gu = jnp.concatenate([hidden_units(w_gate), hidden_units(w_up)], axis=1)
    own_gu = lax.all_gather(after(own_gu, pack), SHARD, axis=0, tiled=True)

    def of_positions(line, y_index, core_index):
        grid = line.reshape(2, 4, 2, rows)
        picked = lax.dynamic_index_in_dim(grid, y_index, 0, keepdims=False)
        picked = lax.dynamic_index_in_dim(picked, core_index, 1, keepdims=False)
        double = jnp.concatenate([picked, picked], axis=0)
        return lax.dynamic_slice_in_dim(double, x_at, 4, axis=0).reshape(-1)

    corners = ((y_at, core), (y_at, 1 - core), (1 - y_at, core), (1 - y_at, 1 - core))
    seg_query = of_positions(seq_ids[0], y_at, core)
    blk_query = of_positions(block_ids[0], y_at, core)
    seg_keys = jnp.concatenate([of_positions(seq_ids[0], *corner) for corner in corners])
    blk_keys = jnp.concatenate([of_positions(block_ids[0], *corner) for corner in corners])
    allowed = (seg_query[:, None] == seg_keys[None, :]) & (blk_keys[None, :] <= blk_query[:, None])
    bias = jnp.where(allowed, 0.0, NEG).astype(F32)
    allowed = (seg_query[None, :] == seg_keys[:, None]) & (blk_keys[:, None] <= blk_query[None, :])
    bias_t = jnp.where(allowed, 0.0, NEG).astype(F32)
    position = of_positions(jnp.arange(seq_ids.shape[1], dtype=jnp.int32), y_at, core)
    freqs = 10000.0 ** (-(jnp.arange(HD // 2).astype(F32) * 2.0 / HD))
    angle = position.astype(F32)[:, None] * freqs[None, :]
    cosine = jnp.concatenate([jnp.cos(angle), jnp.cos(angle)], axis=-1)
    sine = jnp.concatenate([jnp.sin(angle), jnp.sin(angle)], axis=-1)

    count = x_all.shape[0]
    x_all = jnp.concatenate([x_all, x_all[: 3 * rows]], axis=0)
    x_all = lax.dynamic_slice_in_dim(x_all, x_at * rows, count, axis=0).astype(F32)
    top_chunks = gather_x(after(own_top, x_all))
    x_unit = x_all * norm_root(x_all)
    normed_attn = half(x_unit * gain_attn)
    root_attn = norm_root(xval)
    packs_qkv = pack[:, :384], swap_cores(pack[:, :384])
    packs_out = pack[:, 384:], swap_cores(pack[:, 384:])
    own_pre, other_pre = [mm(normed_attn, part) for part in packs_qkv]
    key_pre = jnp.where(first, own_pre[:, 256:], other_pre[:, 256:])
    value_pre = jnp.where(first, other_pre[:, 256:], own_pre[:, 256:])
    query = jnp.concatenate(
        [half(rotate(pre[:, s : s + HD], cosine, sine)) for pre in (own_pre, other_pre) for s in (0, HD)],
        axis=1,
    )
    keys_values = jnp.concatenate([half(rotate(key_pre, cosine, sine)), half(value_pre)], axis=1)
    two_kv = jnp.concatenate([keys_values, across_y(keys_values)], axis=0)
    other_kv = swap_cores(two_kv)
    all_kv = jnp.concatenate(
        [two_kv[:count], other_kv[:count], two_kv[count:], other_kv[count:]], axis=0
    )
    all_keys, all_values = all_kv[:, :HD], all_kv[:, HD:]
    d_ffn = half(keep * jnp.concatenate(top_chunks, axis=0).astype(F32))

    keys_t = all_keys.T
    heads_f, heads, lse = attend(query, keys_t, all_values, bias)

    def chunked(value):
        return [value[j * rows : (j + 1) * rows] for j in range(4)]

    heads = after(heads, d_ffn)
    attn_branch = mm_nt(heads[:, :256], packs_out[0]) + mm_nt(heads[:, 256:], packs_out[1])
    attn_branch = scatter_x(chunked(attn_branch))
    middle = xval + keep * attn_branch
    root_ffn = norm_root(middle)
    normed_ffn = jnp.concatenate(gather_x(half(middle * root_ffn * gain_ffn)), axis=0)

    own_gu, own_down = after(own_gu, normed_ffn), after(own_down, normed_ffn)
    full_gu = (own_gu, swap_cores(own_gu))
    full_down = (own_down, swap_cores(own_down))
    branch = 0.0
    d_normed = 0.0
    d_gus, hiddens = [], []
    for wgu, wd in zip(full_gu, full_down, strict=True):
        gate_up = mm(normed_ffn, wgu)
        gate, up = gate_up[:, :split], gate_up[:, split:]
        sig = jax.nn.sigmoid(gate)
        silu = gate * sig
        hidden = half(silu * up)
        d_hidden = mm(d_ffn, wd)
        d_gate = half(d_hidden * up * sig * (1.0 + gate * (1.0 - sig)))
        d_up = half(d_hidden * silu)
        d_gu = jnp.concatenate([d_gate, d_up], axis=1)
        d_normed = d_normed + mm_nt(d_gu, wgu)
        branch = branch + mm_nt(hidden, wd)
        d_gus.append(d_gu)
        hiddens.append(hidden)
    left_down = after(d_ffn, d_normed)
    grads_down = [mm_tn(left_down, hidden) for hidden in hiddens]
    d_normed_ffn = scatter_x(chunked(d_normed))
    left_gu = after(normed_ffn, d_normed_ffn)
    grads_gu = [mm_tn(left_gu, d_gu) for d_gu in d_gus]
    d_middle = grad_top + norm_backward(middle, root_ffn, gain_ffn, d_normed_ffn)
    gain_ffn_local = jnp.sum(d_normed_ffn * middle * root_ffn, axis=0)

    def both_cores(value):
        other = swap_cores(value)
        return jnp.concatenate(
            [jnp.where(first, value, other), jnp.where(first, other, value)], axis=0
        )

    def sum_cores(mine, theirs):
        return half(mine + swap_cores(half(theirs)).astype(F32))

    def reduce_rows(value):
        return lax.psum_scatter(value, SHARD, scatter_dimension=0, tiled=True)

    def columns(value):
        value = half(value.astype(F32) + across_y(value).astype(F32))
        return absolute(gather_x(value), x_at)

    def units_of(parts, start):
        main = [part[:, start : start + tiles].astype(F32) for part in parts]
        rest = [part[:, start + tiles : start + units].astype(F32) for part in parts]
        return jnp.concatenate(main + rest, axis=1)

    sum_down, sum_gu = sum_cores(*grads_down), sum_cores(*grads_gu)
    own_d_attn = half(keep * d_middle)
    own_d_attn = after(own_d_attn, sum_down)
    d_attn = jnp.concatenate(gather_x(own_d_attn), axis=0)
    rows_down = reduce_rows(sum_down)
    rows_gu = reduce_rows(sum_gu)
    d_attn = after(d_attn, rows_down, sum_gu)
    parts_down = columns(after(rows_down, d_attn))
    ffn_branch = scatter_x(chunked(after(branch, d_attn)))
    output = both_cores(half(middle + keep * ffn_branch))

    d_heads = jnp.concatenate([half(mm(d_attn, part)) for part in packs_out], axis=1)
    delta = jnp.sum((d_heads.astype(F32) * heads_f).reshape(count, 4, HD), axis=-1).T[:, None, :]
    grad_qt, key_part, value_part = attend_back(
        query, query.T, d_heads, d_heads.T, lse.reshape(4, 1, count), delta,
        all_keys, keys_t, all_values, bias_t,
    )
    grad_q = grad_qt.T
    kv_part = jnp.concatenate([key_part, value_part], axis=1)
    kv_mine = jnp.concatenate([kv_part[:count], kv_part[2 * count : 3 * count]], axis=0)
    kv_theirs = jnp.concatenate([kv_part[count : 2 * count], kv_part[3 * count :]], axis=0)
    kv_two = kv_mine + swap_cores(half(kv_theirs)).astype(F32)
    grad_kv = kv_two[:count] + across_y(half(kv_two[count:])).astype(F32)
    grad_kv = after(grad_kv, ffn_branch, *parts_down)
    d_q = [half(unrotate(grad_q[:, h * HD : (h + 1) * HD], cosine, sine)) for h in range(4)]
    d_key = half(unrotate(grad_kv[:, :HD], cosine, sine))
    d_value = half(grad_kv[:, HD:])
    d_own = jnp.concatenate([d_q[0], d_q[1], jnp.where(first, d_key, d_value)], axis=1)
    d_other = jnp.concatenate([d_q[2], d_q[3], jnp.where(first, d_value, d_key)], axis=1)
    d_normed_part = mm_nt(d_own, packs_qkv[0]) + mm_nt(d_other, packs_qkv[1])
    d_normed_attn = scatter_x(chunked(d_normed_part))
    grad_down = units_of(parts_down, 0)
    input_part = norm_backward(xval, root_attn, gain_attn, d_normed_attn)
    input_grad = both_cores(half(d_middle + input_part))
    gain_attn_local = jnp.sum(d_normed_part * x_unit, axis=0)
    gains = half(jnp.stack([gain_attn_local, gain_ffn_local])).T
    sum_qkv = sum_cores(mm_tn(normed_attn, d_own), mm_tn(normed_attn, d_other))
    sum_out = sum_cores(mm_tn(d_attn, heads[:, :256]), mm_tn(d_attn, heads[:, 256:]))
    sums = jnp.concatenate([sum_qkv, sum_out], axis=1)
    sums = jnp.concatenate([sums, jnp.pad(gains, ((0, 0), (0, HD - 2)))], axis=1)
    sixteenth = width // 16
    parts = lax.all_to_all(sums.reshape(16, sixteenth, -1), ("yl", "z", "yh"), 0, 0)
    total_rows = after(half(jnp.sum(parts.astype(F32), axis=0)), rows_gu)
    packs = lax.all_to_all(jnp.broadcast_to(total_rows[None], (8, *total_rows.shape)), ("yh", "x"), 0, 0)
    packs = packs.reshape(2, 4, sixteenth, -1).transpose(1, 0, 2, 3).reshape(4, 2 * sixteenth, -1)
    parts_gu = columns(after(rows_gu, total_rows))
    grad_gate, grad_up = units_of(parts_gu, 0), units_of(parts_gu, split)
    gains = jnp.sum(packs[:, :, 640:642].astype(F32), axis=0)
    gains = (gains + swap_cores(gains)).T
    packs = packs[:, :, :640]
    mine = lax.dynamic_slice_in_dim(packs, 2 * core, 2, axis=0)
    theirs = swap_cores(lax.dynamic_slice_in_dim(packs, 2 - 2 * core, 2, axis=0))
    out0 = jnp.where(first, mine, theirs).astype(F32)
    out1 = jnp.where(first, theirs, mine).astype(F32)
    grad_query = jnp.concatenate(
        [out0[0, :, :256], out1[0, :, :256], out0[1, :, :256], out1[1, :, :256]], axis=1
    )
    grad_key = jnp.concatenate([out0[0, :, 256:384], out0[1, :, 256:384]], axis=1)
    grad_value = jnp.concatenate([out1[0, :, 256:384], out1[1, :, 256:384]], axis=1)
    grad_out = jnp.concatenate(
        [out0[0, :, 384:], out1[0, :, 384:], out0[1, :, 384:], out1[1, :, 384:]], axis=1
    )
    return (
        output[None], input_grad[None], gains[0], gains[1],
        grad_query, grad_key, grad_value, grad_out, grad_gate, grad_up, grad_down,
    )


def solution(mesh):
    fine = Mesh(mesh.devices.reshape(2, 4, 2, 4, 2), ("yl", "z", "yh", "x", "tp"))
    shard, ctx = ("yl", "z"), ("yh", "x")
    acts, weight = P(shard, ctx, None), P(shard, "tp")
    return jax.shard_map(
        per_device,
        mesh=fine,
        in_specs=(acts, acts, P(shard, None), P(shard, None), P(shard), P(), P()) + (weight,) * 7,
        out_specs=(acts, acts, P(shard), P(shard)) + (weight,) * 7,
        check_vma=False,
    )
```

```python
import functools

import jax
import jax.numpy as jnp
from jax import lax
from jax.experimental import pallas as pl
from jax.experimental.pallas import tpu as pltpu
from jax.sharding import Mesh, PartitionSpec as P

HD = 128
EPS = 1e-05
NEG = -1e30
F32 = jnp.float32
BF16 = jnp.bfloat16
SHARD = ("yl", "z")
SCALE = HD ** (-0.5)
LOG2E = 1.4426950408889634
VMEM = 48 * 2**20
SWAP = ((0, 1), (1, 0))


def half(value):
    return value.astype(BF16)


def mm(left, right):
    return jnp.dot(left, right, preferred_element_type=F32)


def mm_nt(left, right):
    return lax.dot_general(left, right, (((1,), (1,)), ((), ())), preferred_element_type=F32)


def mm_tn(left, right):
    return lax.dot_general(left, right, (((0,), (0,)), ((), ())), preferred_element_type=F32)


def swap_cores(value, name="swap"):
    with jax.named_scope(name):
        return lax.ppermute(value, "tp", SWAP)


def across_y(value):
    return lax.ppermute(value, "yh", SWAP)


def after(value, *others):
    zero = sum((other[:1, :1] * 0).astype(value.dtype) for other in others)
    tile = value[:16, :HD] + zero
    return lax.dynamic_update_slice(value, tile, (0, 0))


def shift_x(value, hop):
    return lax.ppermute(value, "x", [(i, (i + hop) % 4) for i in range(4)])


def chunk(value, index):
    rows = value.shape[0] // 4
    return lax.dynamic_slice_in_dim(value, index % 4 * rows, rows, axis=0)


def gather_x(value, name):
    x_at = lax.axis_index("x")
    with jax.named_scope(name):
        moved = {hop: shift_x(value, -hop) for hop in (2, 1, 3)}
    chunks = [value, moved[1], moved[2], moved[3]]
    return [lax.select_n((i - x_at) % 4, *chunks) for i in range(4)]


def scatter_x(value, name):
    x_at = lax.axis_index("x")
    with jax.named_scope(name):
        moved = [shift_x(half(chunk(value, x_at + hop)), hop) for hop in (2, 1, 3)]
    return chunk(value, x_at) + sum(part.astype(F32) for part in moved)


def gather_x_async(value, name):
    with jax.named_scope(name):
        return lax.all_gather(value, "x", axis=0, tiled=True)


def scatter_x_async(value, name):
    with jax.named_scope(name):
        return lax.psum_scatter(half(value), "x", scatter_dimension=0, tiled=True).astype(F32)


def gather_shard(value):
    spread = jnp.broadcast_to(value[None], (8, *value.shape))
    return lax.all_to_all(spread, SHARD, 0, 0).reshape(-1, value.shape[1])


def rotate(value, cosine, sine):
    turned = jnp.concatenate([-value[..., HD // 2 :], value[..., : HD // 2]], axis=-1)
    return value * cosine + turned * sine


def unrotate(grad, cosine, sine):
    scaled = grad * sine
    return grad * cosine + jnp.concatenate(
        [scaled[..., HD // 2 :], -scaled[..., : HD // 2]], axis=-1
    )


def norm_root(value):
    return lax.rsqrt(jnp.mean(value * value, axis=-1, keepdims=True) + EPS)


def norm_backward(value, root, gain, grad):
    scaled = gain * grad
    return root * scaled - value * root**3 * jnp.mean(scaled * value, axis=-1, keepdims=True)


def attend_kernel(q_ref, kt_ref, v_ref, rows_ref, cols_ref, mixed_ref, heads_ref, lse_ref, bias_ref):
    @pl.when(pl.program_id(1) == 0)
    def _():
        seg, blk = rows_ref[:, :1], rows_ref[:, 1:2]
        visible = (seg == cols_ref[:1, :]) & (cols_ref[1:2, :] <= blk)
        bias_ref[...] = jnp.where(visible, 0.0, NEG)

    raw = mm(q_ref[...], kt_ref[...])
    raw = raw * (SCALE * LOG2E) + bias_ref[...]
    top = jnp.max(raw, axis=-1, keepdims=True)
    weights = jnp.exp2(raw - top)
    total = jnp.sum(weights, axis=-1, keepdims=True)
    mixed = mm(half(weights), v_ref[...]) / total
    mixed_ref[...] = mixed
    heads_ref[...] = half(mixed)
    lse = jnp.broadcast_to(top + jnp.log2(total), mixed.shape)
    lse_ref[0] = lse.T[:8, :]


def attend(query, keys_t, values, query_tags, key_tags_t, rows=256):
    count, features = query.shape
    n = values.shape[0]
    part = pl.BlockSpec((rows, HD), lambda j, h: (j, h))
    return pl.pallas_call(
        attend_kernel,
        grid=(count // rows, features // HD),
        in_specs=[
            part,
            pl.BlockSpec((HD, n), lambda j, h: (0, 0)),
            pl.BlockSpec((n, HD), lambda j, h: (0, 0)),
            pl.BlockSpec((rows, 2), lambda j, h: (j, 0)),
            pl.BlockSpec((2, n), lambda j, h: (0, 0)),
        ],
        out_specs=[part, part, pl.BlockSpec((1, 8, rows), lambda j, h: (h, 0, j))],
        out_shape=[
            jax.ShapeDtypeStruct((count, features), F32),
            jax.ShapeDtypeStruct((count, features), BF16),
            jax.ShapeDtypeStruct((features // HD, 8, count), F32),
        ],
        scratch_shapes=[pltpu.VMEM((rows, n), F32)],
        compiler_params=pltpu.CompilerParams(vmem_limit_bytes=VMEM),
    )(query, keys_t, values, query_tags, key_tags_t)


def attend_back_kernel(
    q_ref, do_ref, mixed_ref, lse_ref, k_ref, kt_ref, v_ref, rows_ref, cols_ref, cos_ref, sin_ref,
    dq_ref, dk_ref, dv_ref, bias_ref, *, piece,
):
    @pl.when(pl.program_id(0) == 0)
    def _():
        dk_ref[...] = jnp.zeros_like(dk_ref)
        dv_ref[...] = jnp.zeros_like(dv_ref)
        seg, blk = rows_ref[:, :1], rows_ref[:, 1:2]
        visible = (seg == cols_ref[:1, :]) & (blk <= cols_ref[1:2, :])
        bias_ref[...] = jnp.where(visible, 0.0, NEG)

    q, d_out = q_ref[...], do_ref[...]
    wide = d_out.astype(F32)
    d_out_t = half(wide.T)
    qt = half(q.astype(F32).T)
    delta = jnp.sum((wide * mixed_ref[...]).T, axis=0, keepdims=True)
    lse = lse_ref[0, :1, :]
    grad_qt = jnp.zeros(qt.shape, F32)
    for at in range(0, k_ref.shape[0], piece):
        part = pl.ds(at, piece)
        raw = mm(k_ref[part, :], qt)
        probs = jnp.exp2(raw * (SCALE * LOG2E) + (bias_ref[part, :] - lse))
        d_probs = mm(v_ref[part, :], d_out_t)
        dv_ref[part, :] += mm(half(probs), d_out)
        d_scores = half(probs * (SCALE * (d_probs - delta)))
        dk_ref[part, :] += mm(d_scores, q)
        grad_qt += mm(kt_ref[:, part], d_scores)
    grad_q = grad_qt.T
    scaled = grad_q * sin_ref[...]
    lane = lax.broadcasted_iota(jnp.int32, scaled.shape, 1)
    turned = pltpu.roll(scaled, HD // 2, 1)
    dq_ref[...] = half(grad_q * cos_ref[...] + jnp.where(lane < HD // 2, turned, -turned))


def attend_back(query, d_heads, mixed, lse, keys, keys_t, values, key_tags, query_tags_t, cosine, sine):
    count, features = query.shape
    n = keys.shape[0]
    row = pl.BlockSpec((count, HD), lambda h: (0, h))

    def whole(*shape):
        return pl.BlockSpec(shape, lambda h: (0, 0))

    return pl.pallas_call(
        functools.partial(attend_back_kernel, piece=min(512, n)),
        grid=(features // HD,),
        in_specs=[
            row, row, row, pl.BlockSpec((1, 8, count), lambda h: (h, 0, 0)), whole(n, HD),
            whole(HD, n), whole(n, HD), whole(n, 2), whole(2, count), whole(count, HD), whole(count, HD),
        ],
        out_specs=[row, whole(n, HD), whole(n, HD)],
        out_shape=[
            jax.ShapeDtypeStruct((count, features), BF16),
            jax.ShapeDtypeStruct((n, HD), F32),
            jax.ShapeDtypeStruct((n, HD), F32),
        ],
        scratch_shapes=[pltpu.VMEM((n, count), F32)],
        compiler_params=pltpu.CompilerParams(vmem_limit_bytes=VMEM),
    )(query, d_heads, mixed, lse, keys, keys_t, values, key_tags, query_tags_t, cosine, sine)


def spread_kernel(parts_ref, *out_refs, tiles, spare):
    split = tiles + HD
    for place, out_ref in enumerate(out_refs):
        at = place * split
        for i in range(4):
            out_ref[:, i * tiles : (i + 1) * tiles] = parts_ref[i, :, at : at + tiles].astype(F32)
        rest = [parts_ref[i, :, at + tiles : at + split].astype(F32) for i in range(4)]
        for i in (0, 2):
            start = 4 * tiles + i * spare
            out_ref[:, start : start + HD] = rest[i] + pltpu.roll(rest[i + 1], spare, 1)


def spread(parts, tiles, spare, rows=64):
    _, count, columns = parts.shape
    outs = columns // (tiles + HD)
    units = 4 * (tiles + spare)
    return pl.pallas_call(
        functools.partial(spread_kernel, tiles=tiles, spare=spare),
        grid=(count // rows,),
        in_specs=[pl.BlockSpec((4, rows, columns), lambda j: (0, j, 0))],
        out_specs=[pl.BlockSpec((rows, units), lambda j: (j, 0))] * outs,
        out_shape=[jax.ShapeDtypeStruct((count, units), F32)] * outs,
        compiler_params=pltpu.CompilerParams(vmem_limit_bytes=VMEM),
    )(parts)


def per_device(
    tokens, cotangent, seq_ids, block_ids, keep_layer, gain_attn, gain_ffn,
    w_query, w_key, w_value, w_out, w_gate, w_up, w_down,
):
    core, x_at, y_at = lax.axis_index("tp"), lax.axis_index("x"), lax.axis_index("yh")
    first = core == 0
    rows = tokens.shape[1] // 2
    width = tokens.shape[2]
    keep = keep_layer[0].astype(F32)

    own_tokens = lax.dynamic_slice_in_dim(tokens[0], core * rows, rows, axis=0)
    own_top = lax.dynamic_slice_in_dim(cotangent[0], core * rows, rows, axis=0)
    x_top = gather_x_async(jnp.concatenate([own_tokens, own_top], axis=0), "token_gather")
    x_top = x_top.reshape(4, 2, rows, width)
    x_all, top_all = x_top[:, 0].reshape(-1, width), x_top[:, 1].reshape(-1, width)
    xval, grad_top = own_tokens.astype(F32), own_top.astype(F32)

    side = x_at // 2
    at = x_at % 2
    wq = half(lax.dynamic_slice_in_dim(w_query, at * 512, 512, axis=1))
    wk = half(lax.dynamic_slice_in_dim(w_key, at * HD, HD, axis=1))
    wv = half(lax.dynamic_slice_in_dim(w_value, at * HD, HD, axis=1))
    wo = half(lax.dynamic_slice_in_dim(w_out, at * 512, 512, axis=1))
    pack0 = jnp.concatenate([wq[:, :256], wk, wo[:, :256]], axis=1)
    pack1 = jnp.concatenate([wq[:, 256:], wv, wo[:, 256:]], axis=1)
    lent = lax.ppermute(
        jnp.where(first, pack1, pack0),
        ("x", "tp"),
        [(2 * i + i // 2, 2 * i + 1 - i // 2) for i in range(4)],
    )
    pack = jnp.where(core == side, jnp.where(first, pack0, pack1), lent)
    pack = gather_shard(pack)

    units = w_gate.shape[1] // 4
    tiles = units // HD * HD
    spare = units - tiles
    split = tiles + HD

    def hidden_units(weight):
        main = lax.dynamic_slice_in_dim(weight, x_at * tiles, tiles, axis=1)
        rest = lax.dynamic_slice_in_dim(weight[:, 4 * tiles :], x_at * spare, spare, axis=1)
        return jnp.concatenate([half(main), jnp.pad(half(rest), ((0, 0), (0, HD - spare)))], axis=1)

    own_ffn = jnp.concatenate([hidden_units(w) for w in (w_gate, w_up, w_down)], axis=1)
    with jax.named_scope("unit_gather"):
        own_ffn = lax.all_gather(after(own_ffn, pack), SHARD, axis=0, tiled=True)

    def of_positions(line, y_index, core_index):
        grid = line.reshape(2, 4, 2, rows)
        picked = lax.dynamic_index_in_dim(grid, y_index, 0, keepdims=False)
        picked = lax.dynamic_index_in_dim(picked, core_index, 1, keepdims=False)
        return picked.reshape(-1)

    corners = ((y_at, core), (y_at, 1 - core), (1 - y_at, core), (1 - y_at, 1 - core))
    lines = (seq_ids[0], block_ids[0])
    query_tags_t = jnp.stack([of_positions(line, y_at, core) for line in lines])
    key_tags_t = jnp.stack(
        [jnp.concatenate([of_positions(line, *corner) for corner in corners]) for line in lines]
    )
    query_tags, key_tags = query_tags_t.T, key_tags_t.T
    position = of_positions(jnp.arange(seq_ids.shape[1], dtype=jnp.int32), y_at, core)
    freqs = 10000.0 ** (-(jnp.arange(HD // 2).astype(F32) * 2.0 / HD))
    angle = position.astype(F32)[:, None] * freqs[None, :]
    cosine = jnp.concatenate([jnp.cos(angle), jnp.cos(angle)], axis=-1)
    sine = jnp.concatenate([jnp.sin(angle), jnp.sin(angle)], axis=-1)

    count = x_all.shape[0]
    x_all = x_all.astype(F32)
    x_unit = x_all * norm_root(x_all)
    normed_attn = half(x_unit * gain_attn)
    root_attn = norm_root(xval)
    packs_qkv = pack[:, :384], swap_cores(pack[:, :384])
    packs_out = pack[:, 384:], swap_cores(pack[:, 384:])
    own_pre, other_pre = [mm(normed_attn, part) for part in packs_qkv]
    key_pre = jnp.where(first, own_pre[:, 256:], other_pre[:, 256:])
    value_pre = jnp.where(first, other_pre[:, 256:], own_pre[:, 256:])
    query = jnp.concatenate(
        [half(rotate(pre[:, s : s + HD], cosine, sine)) for pre in (own_pre, other_pre) for s in (0, HD)],
        axis=1,
    )
    keys_values = jnp.concatenate([half(rotate(key_pre, cosine, sine)), half(value_pre)], axis=1)
    two_kv = jnp.concatenate([keys_values, across_y(keys_values)], axis=0)
    other_kv = swap_cores(two_kv)
    all_kv = jnp.concatenate(
        [two_kv[:count], other_kv[:count], two_kv[count:], other_kv[count:]], axis=0
    )
    all_keys, all_values = all_kv[:, :HD], all_kv[:, HD:]
    d_ffn = half(keep * top_all.astype(F32))

    keys_t = all_keys.T
    heads_f, heads, lse = attend(query, keys_t, all_values, query_tags, key_tags_t)

    attn_branch = mm_nt(heads[:, :256], packs_out[0]) + mm_nt(heads[:, 256:], packs_out[1])
    attn_branch = scatter_x(attn_branch, "attn_scatter")
    middle = xval + keep * attn_branch
    root_ffn = norm_root(middle)
    normed_ffn = jnp.concatenate(gather_x(half(middle * root_ffn * gain_ffn), "ffn_gather"), axis=0)

    own_ffn = after(own_ffn, normed_ffn)
    other_ffn = swap_cores(own_ffn)
    full_gu = (own_ffn[:, : 2 * split], other_ffn[:, : 2 * split])
    full_down = (own_ffn[:, 2 * split :], other_ffn[:, 2 * split :])
    branch = 0.0
    d_normed = 0.0
    d_gus, hiddens = [], []
    for wgu, wd in zip(full_gu, full_down, strict=True):
        gate_up = mm(after(normed_ffn, *hiddens[-1:]), wgu)
        gate, up = gate_up[:, :split], gate_up[:, split:]
        sig = jax.nn.sigmoid(gate)
        silu = gate * sig
        hidden = half(silu * up)
        d_hidden = mm(d_ffn, wd)
        d_gate = half(d_hidden * up * sig * (1.0 + gate * (1.0 - sig)))
        d_up = half(d_hidden * silu)
        d_gu = jnp.concatenate([d_gate, d_up], axis=1)
        d_normed = d_normed + mm_nt(d_gu, wgu)
        branch = branch + mm_nt(hidden, wd)
        d_gus.append(d_gu)
        hiddens.append(hidden)
    grads_down = [mm_tn(d_ffn, hidden) for hidden in hiddens]
    d_normed_ffn = scatter_x(d_normed, "d_ffn_scatter")
    left_gu = after(normed_ffn, d_normed_ffn)
    grads_gu = [mm_tn(left_gu, d_gu) for d_gu in d_gus]
    d_middle = grad_top + norm_backward(middle, root_ffn, gain_ffn, d_normed_ffn)
    gain_ffn_local = jnp.sum(d_normed_ffn * middle * root_ffn, axis=0)

    def both_cores(value):
        other = swap_cores(value)
        return jnp.concatenate(
            [jnp.where(first, value, other), jnp.where(first, other, value)], axis=0
        )

    def sum_cores(mine, theirs):
        return half(mine + swap_cores(half(theirs)).astype(F32))

    def reduce_rows(value, name):
        with jax.named_scope(name + "_rows"):
            parts = lax.all_to_all(value.reshape(16, width // 16, -1), ("yl", "z", "yh"), 0, 0)
        return half(jnp.sum(parts.astype(F32), axis=0))

    def columns(value, name):
        spread = jnp.broadcast_to(value[None], (8, *value.shape))
        with jax.named_scope(name + "_columns"):
            parts = lax.all_to_all(spread, ("yh", "x"), 0, 0)
        return parts.reshape(2, 4, *value.shape)

    def rows_of(parts, x_index):
        return parts[:, x_index].reshape(-1, parts.shape[-1])

    def samples(value, name):
        with jax.named_scope(name + "_rows"):
            return lax.psum_scatter(value, SHARD, scatter_dimension=0, tiled=True)

    def halves(value, name):
        with jax.named_scope(name + "_y"):
            return half(value.astype(F32) + across_y(value).astype(F32))

    sum_down, sum_gu = sum_cores(*grads_down), sum_cores(*grads_gu)
    rows_down = samples(sum_down, "down")
    d_attn = gather_x_async(after(half(keep * d_middle), rows_down), "d_attn_gather")
    rows_gu = samples(after(sum_gu, d_attn), "gate_up")
    d_attn = after(d_attn, branch)
    unit_down = halves(after(rows_down, d_attn), "down")
    ffn_branch = scatter_x(after(branch, d_attn), "branch_scatter")
    output = both_cores(half(middle + keep * ffn_branch))

    d_heads = jnp.concatenate([half(mm(d_attn, part)) for part in packs_out], axis=1)
    d_query, key_part, value_part = attend_back(
        query, d_heads, heads_f, lse, all_keys, keys_t, all_values, key_tags, query_tags_t, cosine, sine
    )
    kv_part = jnp.concatenate([key_part, value_part], axis=1)
    kv_mine = jnp.concatenate([kv_part[:count], kv_part[2 * count : 3 * count]], axis=0)
    kv_theirs = jnp.concatenate([kv_part[count : 2 * count], kv_part[3 * count :]], axis=0)
    kv_two = kv_mine + swap_cores(half(kv_theirs)).astype(F32)
    grad_kv = kv_two[:count] + across_y(half(kv_two[count:])).astype(F32)
    grad_kv = after(grad_kv, ffn_branch, unit_down)
    d_key = half(unrotate(grad_kv[:, :HD], cosine, sine))
    d_value = half(grad_kv[:, HD:])
    d_own = jnp.concatenate([d_query[:, :256], jnp.where(first, d_key, d_value)], axis=1)
    d_other = jnp.concatenate([d_query[:, 256:], jnp.where(first, d_value, d_key)], axis=1)
    d_normed_part = mm_nt(d_own, packs_qkv[0]) + mm_nt(d_other, packs_qkv[1])
    d_normed_attn = scatter_x_async(d_normed_part, "d_attn_scatter")
    input_part = norm_backward(xval, root_attn, gain_attn, d_normed_attn)
    input_grad = both_cores(half(d_middle + input_part))
    gain_attn_local = jnp.sum(d_normed_part * x_unit, axis=0)
    gains = half(jnp.stack([gain_attn_local, gain_ffn_local])).T
    sum_qkv = sum_cores(mm_tn(normed_attn, d_own), mm_tn(normed_attn, d_other))
    sum_out = sum_cores(mm_tn(d_attn, heads[:, :256]), mm_tn(d_attn, heads[:, 256:]))
    sums = jnp.concatenate([sum_qkv, sum_out], axis=1)
    sums = jnp.concatenate([sums, jnp.pad(gains, ((0, 0), (0, HD - 2)))], axis=1)
    total_rows = after(reduce_rows(sums, "attn"), rows_gu)
    packs = columns(total_rows, "attn")
    unit_rows = jnp.concatenate([halves(rows_gu, "gate_up"), unit_down], axis=1)
    with jax.named_scope("unit_columns"):
        parts = lax.all_gather(unit_rows, "x", axis=0, tiled=False)
    grad_gate, grad_up, grad_down = spread(parts, tiles, spare)
    packs = jnp.stack([rows_of(packs, i) for i in range(4)])
    gains = jnp.sum(packs[:, :, 640:642].astype(F32), axis=0)
    gains = (gains + swap_cores(gains)).T
    packs = packs[:, :, :640]
    mine = lax.dynamic_slice_in_dim(packs, 2 * core, 2, axis=0)
    theirs = swap_cores(lax.dynamic_slice_in_dim(packs, 2 - 2 * core, 2, axis=0))
    out0 = jnp.where(first, mine, theirs).astype(F32)
    out1 = jnp.where(first, theirs, mine).astype(F32)
    grad_query = jnp.concatenate(
        [out0[0, :, :256], out1[0, :, :256], out0[1, :, :256], out1[1, :, :256]], axis=1
    )
    grad_key = jnp.concatenate([out0[0, :, 256:384], out0[1, :, 256:384]], axis=1)
    grad_value = jnp.concatenate([out1[0, :, 256:384], out1[1, :, 256:384]], axis=1)
    grad_out = jnp.concatenate(
        [out0[0, :, 384:], out1[0, :, 384:], out0[1, :, 384:], out1[1, :, 384:]], axis=1
    )
    return (
        output[None], input_grad[None], gains[0], gains[1],
        grad_query, grad_key, grad_value, grad_out, grad_gate, grad_up, grad_down,
    )


def solution(mesh):
    fine = Mesh(mesh.devices.reshape(2, 4, 2, 4, 2), ("yl", "z", "yh", "x", "tp"))
    shard, ctx = ("yl", "z"), ("yh", "x")
    acts, weight = P(shard, ctx, None), P(shard, "tp")
    return jax.shard_map(
        per_device,
        mesh=fine,
        in_specs=(acts, acts, P(shard, None), P(shard, None), P(shard), P(), P()) + (weight,) * 7,
        out_specs=(acts, acts, P(shard), P(shard)) + (weight,) * 7,
        check_vma=False,
    )
```

```python
import functools

import jax
import jax.numpy as jnp
from jax import lax
from jax.experimental import pallas as pl
from jax.experimental.pallas import tpu as pltpu
from jax.sharding import Mesh, PartitionSpec as P

HD = 128
EPS = 1e-05
NEG = -1e30
F32 = jnp.float32
BF16 = jnp.bfloat16
SHARD = ("yl", "z")
SCALE = HD ** (-0.5)
LOG2E = 1.4426950408889634
VMEM = 48 * 2**20
SWAP = ((0, 1), (1, 0))


def half(value):
    return value.astype(BF16)


def mm(left, right):
    return jnp.dot(left, right, preferred_element_type=F32)


def mm_nt(left, right):
    return lax.dot_general(left, right, (((1,), (1,)), ((), ())), preferred_element_type=F32)


def mm_tn(left, right):
    return lax.dot_general(left, right, (((0,), (0,)), ((), ())), preferred_element_type=F32)


def swap_cores(value, name="swap"):
    with jax.named_scope(name):
        return lax.ppermute(value, "tp", SWAP)


def across_y(value):
    return lax.ppermute(value, "yh", SWAP)


def after(value, *others):
    zero = sum((other[:1, :1] * 0).astype(value.dtype) for other in others)
    tile = value[:16, :HD] + zero
    return lax.dynamic_update_slice(value, tile, (0, 0))


def shift_x(value, hop):
    return lax.ppermute(value, "x", [(i, (i + hop) % 4) for i in range(4)])


def chunk(value, index):
    rows = value.shape[0] // 4
    return lax.dynamic_slice_in_dim(value, index % 4 * rows, rows, axis=0)


def gather_x(value, name):
    x_at = lax.axis_index("x")
    with jax.named_scope(name):
        moved = {hop: shift_x(value, -hop) for hop in (2, 1, 3)}
    chunks = [value, moved[1], moved[2], moved[3]]
    return [lax.select_n((i - x_at) % 4, *chunks) for i in range(4)]


def scatter_x(value, name):
    x_at = lax.axis_index("x")
    with jax.named_scope(name):
        moved = [shift_x(chunk(value, x_at + hop), hop) for hop in (2, 1, 3)]
    return sum((part.astype(F32) for part in moved), chunk(value, x_at).astype(F32))


def gather_x_async(value, name):
    with jax.named_scope(name):
        return lax.all_gather(value, "x", axis=0, tiled=True)


def scatter_x_async(value, name):
    with jax.named_scope(name):
        return lax.psum_scatter(half(value), "x", scatter_dimension=0, tiled=True).astype(F32)


def gather_shard(value):
    spread = jnp.broadcast_to(value[None], (8, *value.shape))
    return lax.all_to_all(spread, SHARD, 0, 0).reshape(-1, value.shape[1])


def rotate(value, cosine, sine):
    turned = jnp.concatenate([-value[..., HD // 2 :], value[..., : HD // 2]], axis=-1)
    return value * cosine + turned * sine


def unrotate(grad, cosine, sine):
    scaled = grad * sine
    return grad * cosine + jnp.concatenate(
        [scaled[..., HD // 2 :], -scaled[..., : HD // 2]], axis=-1
    )


def norm_root(value):
    return lax.rsqrt(jnp.mean(value * value, axis=-1, keepdims=True) + EPS)


def norm_backward(value, root, gain, grad):
    scaled = gain * grad
    return root * scaled - value * root**3 * jnp.mean(scaled * value, axis=-1, keepdims=True)


def attend_kernel(q_ref, kt_ref, v_ref, rows_ref, cols_ref, mixed_ref, heads_ref, lse_ref, bias_ref):
    @pl.when(pl.program_id(1) == 0)
    def _():
        seg, blk = rows_ref[:, :1], rows_ref[:, 1:2]
        visible = (seg == cols_ref[:1, :]) & (cols_ref[1:2, :] <= blk)
        bias_ref[...] = jnp.where(visible, 0.0, NEG)

    raw = mm(q_ref[...], kt_ref[...])
    raw = raw * (SCALE * LOG2E) + bias_ref[...]
    top = jnp.max(raw, axis=-1, keepdims=True)
    weights = jnp.exp2(raw - top)
    total = jnp.sum(weights, axis=-1, keepdims=True)
    mixed = mm(half(weights), v_ref[...]) / total
    mixed_ref[...] = mixed
    heads_ref[...] = half(mixed)
    lse = jnp.broadcast_to(top + jnp.log2(total), mixed.shape)
    lse_ref[0] = lse.T[:8, :]


def attend(query, keys_t, values, query_tags, key_tags_t, rows=256):
    count, features = query.shape
    n = values.shape[0]
    part = pl.BlockSpec((rows, HD), lambda j, h: (j, h))
    return pl.pallas_call(
        attend_kernel,
        grid=(count // rows, features // HD),
        in_specs=[
            part,
            pl.BlockSpec((HD, n), lambda j, h: (0, 0)),
            pl.BlockSpec((n, HD), lambda j, h: (0, 0)),
            pl.BlockSpec((rows, 2), lambda j, h: (j, 0)),
            pl.BlockSpec((2, n), lambda j, h: (0, 0)),
        ],
        out_specs=[part, part, pl.BlockSpec((1, 8, rows), lambda j, h: (h, 0, j))],
        out_shape=[
            jax.ShapeDtypeStruct((count, features), F32),
            jax.ShapeDtypeStruct((count, features), BF16),
            jax.ShapeDtypeStruct((features // HD, 8, count), F32),
        ],
        scratch_shapes=[pltpu.VMEM((rows, n), F32)],
        compiler_params=pltpu.CompilerParams(vmem_limit_bytes=VMEM),
        cost_estimate=pl.CostEstimate(
            flops=8 * count * features * n, transcendentals=count * features // HD * n, bytes_accessed=2**22
        ),
    )(query, keys_t, values, query_tags, key_tags_t)


def attend_back_kernel(
    q_ref, do_ref, mixed_ref, lse_ref, k_ref, kt_ref, v_ref, rows_ref, cols_ref, cos_ref, sin_ref,
    dq_ref, dk_ref, dv_ref, bias_ref, *, piece,
):
    @pl.when(pl.program_id(0) == 0)
    def _():
        dk_ref[...] = jnp.zeros_like(dk_ref)
        dv_ref[...] = jnp.zeros_like(dv_ref)
        seg, blk = rows_ref[:, :1], rows_ref[:, 1:2]
        visible = (seg == cols_ref[:1, :]) & (blk <= cols_ref[1:2, :])
        bias_ref[...] = jnp.where(visible, 0.0, NEG)

    q, d_out = q_ref[...], do_ref[...]
    wide = d_out.astype(F32)
    d_out_t = half(wide.T)
    qt = half(q.astype(F32).T)
    delta = jnp.sum((wide * mixed_ref[...]).T, axis=0, keepdims=True)
    lse = lse_ref[0, :1, :]
    grad_qt = jnp.zeros(qt.shape, F32)
    for at in range(0, k_ref.shape[0], piece):
        part = pl.ds(at, piece)
        raw = mm(k_ref[part, :], qt)
        probs = jnp.exp2(raw * (SCALE * LOG2E) + (bias_ref[part, :] - lse))
        d_probs = mm(v_ref[part, :], d_out_t)
        dv_ref[part, :] += mm(half(probs), d_out)
        d_scores = half(probs * (SCALE * (d_probs - delta)))
        dk_ref[part, :] += mm(d_scores, q)
        grad_qt += mm(kt_ref[:, part], d_scores)
    grad_q = grad_qt.T
    scaled = grad_q * sin_ref[...]
    lane = lax.broadcasted_iota(jnp.int32, scaled.shape, 1)
    turned = pltpu.roll(scaled, HD // 2, 1)
    dq_ref[...] = half(grad_q * cos_ref[...] + jnp.where(lane < HD // 2, turned, -turned))


def attend_back(query, d_heads, mixed, lse, keys, keys_t, values, key_tags, query_tags_t, cosine, sine):
    count, features = query.shape
    n = keys.shape[0]
    row = pl.BlockSpec((count, HD), lambda h: (0, h))

    def whole(*shape):
        return pl.BlockSpec(shape, lambda h: (0, 0))

    return pl.pallas_call(
        functools.partial(attend_back_kernel, piece=min(512, n)),
        grid=(features // HD,),
        in_specs=[
            row, row, row, pl.BlockSpec((1, 8, count), lambda h: (h, 0, 0)), whole(n, HD),
            whole(HD, n), whole(n, HD), whole(n, 2), whole(2, count), whole(count, HD), whole(count, HD),
        ],
        out_specs=[row, whole(n, HD), whole(n, HD)],
        out_shape=[
            jax.ShapeDtypeStruct((count, features), BF16),
            jax.ShapeDtypeStruct((n, HD), F32),
            jax.ShapeDtypeStruct((n, HD), F32),
        ],
        scratch_shapes=[pltpu.VMEM((n, count), F32)],
        compiler_params=pltpu.CompilerParams(vmem_limit_bytes=VMEM),
        cost_estimate=pl.CostEstimate(
            flops=20 * count * features * n, transcendentals=count * features // HD * n, bytes_accessed=2**23
        ),
    )(query, d_heads, mixed, lse, keys, keys_t, values, key_tags, query_tags_t, cosine, sine)


def place_heads_kernel(core_ref, mine_ref, theirs_ref, q_ref, k_ref, v_ref, o_ref):
    def place(first_ref, second_ref):
        for y in range(2):
            rows = pl.ds(y * first_ref.shape[2], first_ref.shape[2])
            for x in range(2):
                for i, ref in enumerate((first_ref, second_ref)):
                    lane = x * 512 + i * 256
                    q_ref[rows, lane : lane + 256] = ref[y, x, :, :256].astype(F32)
                    o_ref[rows, lane : lane + 256] = ref[y, x, :, 384:].astype(F32)
                k_ref[rows, x * HD : (x + 1) * HD] = first_ref[y, x, :, 256:384].astype(F32)
                v_ref[rows, x * HD : (x + 1) * HD] = second_ref[y, x, :, 256:384].astype(F32)

    @pl.when(core_ref[0] == 0)
    def _():
        place(mine_ref, theirs_ref)

    @pl.when(core_ref[0] != 0)
    def _():
        place(theirs_ref, mine_ref)


def place_heads(core, mine, theirs):
    rows = 2 * mine.shape[2]
    return pl.pallas_call(
        place_heads_kernel,
        in_specs=[
            pl.BlockSpec(memory_space=pltpu.SMEM),
            pl.BlockSpec(memory_space=pltpu.VMEM),
            pl.BlockSpec(memory_space=pltpu.VMEM),
        ],
        out_shape=[jax.ShapeDtypeStruct((rows, columns), F32) for columns in (1024, 256, 256, 1024)],
        compiler_params=pltpu.CompilerParams(vmem_limit_bytes=VMEM),
    )(core.reshape(1).astype(jnp.int32), mine, theirs)


def spread_kernel(parts_ref, *out_refs, tiles, spare):
    split = tiles + HD
    for place, out_ref in enumerate(out_refs):
        at = place * split
        for i in range(4):
            out_ref[:, i * tiles : (i + 1) * tiles] = parts_ref[i, :, at : at + tiles].astype(F32)
        rest = [parts_ref[i, :, at + tiles : at + split].astype(F32) for i in range(4)]
        for i in (0, 2):
            start = 4 * tiles + i * spare
            out_ref[:, start : start + HD] = rest[i] + pltpu.roll(rest[i + 1], spare, 1)


def spread(parts, tiles, spare, rows=64):
    _, count, columns = parts.shape
    outs = columns // (tiles + HD)
    units = 4 * (tiles + spare)
    return pl.pallas_call(
        functools.partial(spread_kernel, tiles=tiles, spare=spare),
        grid=(count // rows,),
        in_specs=[pl.BlockSpec((4, rows, columns), lambda j: (0, j, 0))],
        out_specs=[pl.BlockSpec((rows, units), lambda j: (j, 0))] * outs,
        out_shape=[jax.ShapeDtypeStruct((count, units), F32)] * outs,
        compiler_params=pltpu.CompilerParams(vmem_limit_bytes=VMEM),
    )(parts)


def per_device(
    tokens, cotangent, seq_ids, block_ids, keep_layer, gain_attn, gain_ffn,
    w_query, w_key, w_value, w_out, w_gate, w_up, w_down,
):
    core, x_at, y_at = lax.axis_index("tp"), lax.axis_index("x"), lax.axis_index("yh")
    first = core == 0
    rows = tokens.shape[1] // 2
    width = tokens.shape[2]
    keep = keep_layer[0].astype(F32)

    own_tokens = lax.dynamic_slice_in_dim(tokens[0], core * rows, rows, axis=0)
    own_top = lax.dynamic_slice_in_dim(cotangent[0], core * rows, rows, axis=0)
    x_top = gather_x_async(jnp.concatenate([own_tokens, own_top], axis=0), "token_gather")
    x_top = x_top.reshape(4, 2, rows, width)
    x_all, top_all = x_top[:, 0].reshape(-1, width), x_top[:, 1].reshape(-1, width)
    xval, grad_top = own_tokens.astype(F32), own_top.astype(F32)

    side = x_at // 2
    at = x_at % 2
    wq = half(lax.dynamic_slice_in_dim(w_query, at * 512, 512, axis=1))
    wk = half(lax.dynamic_slice_in_dim(w_key, at * HD, HD, axis=1))
    wv = half(lax.dynamic_slice_in_dim(w_value, at * HD, HD, axis=1))
    wo = half(lax.dynamic_slice_in_dim(w_out, at * 512, 512, axis=1))
    pack0 = jnp.concatenate([wq[:, :256], wk, wo[:, :256]], axis=1)
    pack1 = jnp.concatenate([wq[:, 256:], wv, wo[:, 256:]], axis=1)
    lent = lax.ppermute(
        jnp.where(first, pack1, pack0),
        ("x", "tp"),
        [(2 * i + i // 2, 2 * i + 1 - i // 2) for i in range(4)],
    )
    pack = jnp.where(core == side, jnp.where(first, pack0, pack1), lent)
    pack = gather_shard(pack)

    units = w_gate.shape[1] // 4
    tiles = units // HD * HD
    spare = units - tiles
    split = tiles + HD

    def hidden_units(weight):
        main = lax.dynamic_slice_in_dim(weight, x_at * tiles, tiles, axis=1)
        rest = lax.dynamic_slice_in_dim(weight[:, 4 * tiles :], x_at * spare, spare, axis=1)
        return jnp.concatenate([half(main), jnp.pad(half(rest), ((0, 0), (0, HD - spare)))], axis=1)

    own_ffn = jnp.concatenate([hidden_units(w) for w in (w_gate, w_up, w_down)], axis=1)
    with jax.named_scope("unit_gather"):
        own_ffn = lax.all_gather(after(own_ffn, pack), SHARD, axis=0, tiled=True)

    def of_positions(line, y_index, core_index):
        grid = line.reshape(2, 4, 2, rows)
        picked = lax.dynamic_index_in_dim(grid, y_index, 0, keepdims=False)
        picked = lax.dynamic_index_in_dim(picked, core_index, 1, keepdims=False)
        return picked.reshape(-1)

    corners = ((y_at, core), (y_at, 1 - core), (1 - y_at, core), (1 - y_at, 1 - core))
    lines = (seq_ids[0], block_ids[0])
    query_tags_t = jnp.stack([of_positions(line, y_at, core) for line in lines])
    key_tags_t = jnp.stack(
        [jnp.concatenate([of_positions(line, *corner) for corner in corners]) for line in lines]
    )
    query_tags, key_tags = query_tags_t.T, key_tags_t.T
    position = of_positions(jnp.arange(seq_ids.shape[1], dtype=jnp.int32), y_at, core)
    freqs = 10000.0 ** (-(jnp.arange(HD // 2).astype(F32) * 2.0 / HD))
    angle = position.astype(F32)[:, None] * freqs[None, :]
    cosine = jnp.concatenate([jnp.cos(angle), jnp.cos(angle)], axis=-1)
    sine = jnp.concatenate([jnp.sin(angle), jnp.sin(angle)], axis=-1)

    count = x_all.shape[0]
    x_all = x_all.astype(F32)
    x_unit = x_all * norm_root(x_all)
    normed_attn = half(x_unit * gain_attn)
    root_attn = norm_root(xval)
    packs_qkv = pack[:, :384], swap_cores(pack[:, :384])
    packs_out = pack[:, 384:], swap_cores(pack[:, 384:])
    own_pre, other_pre = [mm(normed_attn, part) for part in packs_qkv]
    key_pre = jnp.where(first, own_pre[:, 256:], other_pre[:, 256:])
    value_pre = jnp.where(first, other_pre[:, 256:], own_pre[:, 256:])
    query = jnp.concatenate(
        [half(rotate(pre[:, s : s + HD], cosine, sine)) for pre in (own_pre, other_pre) for s in (0, HD)],
        axis=1,
    )
    keys_values = jnp.concatenate([half(rotate(key_pre, cosine, sine)), half(value_pre)], axis=1)
    two_kv = jnp.concatenate([keys_values, across_y(keys_values)], axis=0)
    other_kv = swap_cores(two_kv)
    all_kv = jnp.concatenate(
        [two_kv[:count], other_kv[:count], two_kv[count:], other_kv[count:]], axis=0
    )
    all_keys, all_values = all_kv[:, :HD], all_kv[:, HD:]
    d_ffn = half(keep * top_all.astype(F32))

    keys_t = all_keys.T
    heads_f, heads, lse = attend(query, keys_t, all_values, query_tags, key_tags_t)

    attn_branch = mm_nt(heads[:, :256], packs_out[0]) + mm_nt(heads[:, 256:], packs_out[1])
    attn_branch = scatter_x(half(attn_branch), "attn_scatter")
    middle = xval + keep * attn_branch
    root_ffn = norm_root(middle)
    normed_ffn = jnp.concatenate(gather_x(half(middle * root_ffn * gain_ffn), "ffn_gather"), axis=0)

    own_ffn = after(own_ffn, normed_ffn)
    other_ffn = swap_cores(own_ffn)
    full_gu = (own_ffn[:, : 2 * split], other_ffn[:, : 2 * split])
    full_down = (own_ffn[:, 2 * split :], other_ffn[:, 2 * split :])
    branch = 0.0
    d_normed = 0.0
    d_gus, hiddens = [], []
    for wgu, wd in zip(full_gu, full_down, strict=True):
        gate_up = mm(after(normed_ffn, *hiddens[-1:]), wgu)
        gate, up = gate_up[:, :split], gate_up[:, split:]
        sig = jax.nn.sigmoid(gate)
        silu = gate * sig
        hidden = half(silu * up)
        d_hidden = mm(d_ffn, wd)
        d_gate = half(d_hidden * up * sig * (1.0 + gate * (1.0 - sig)))
        d_up = half(d_hidden * silu)
        d_gu = jnp.concatenate([d_gate, d_up], axis=1)
        d_normed = d_normed + mm_nt(d_gu, wgu)
        branch = branch + mm_nt(hidden, wd)
        d_gus.append(d_gu)
        hiddens.append(hidden)
    grads_down = [mm_tn(d_ffn, hidden) for hidden in hiddens]
    d_normed_ffn = scatter_x(half(d_normed), "d_ffn_scatter")
    left_gu = after(normed_ffn, d_normed_ffn)
    grads_gu = [mm_tn(left_gu, d_gu) for d_gu in d_gus]
    d_middle = grad_top + norm_backward(middle, root_ffn, gain_ffn, d_normed_ffn)
    gain_ffn_local = jnp.sum(d_normed_ffn * middle * root_ffn, axis=0)

    def both_cores(value):
        other = swap_cores(value)
        return jnp.concatenate(
            [jnp.where(first, value, other), jnp.where(first, other, value)], axis=0
        )

    def sum_cores(mine, theirs):
        return half(mine + swap_cores(half(theirs)).astype(F32))

    def reduce_rows(value, name):
        with jax.named_scope(name + "_rows"):
            parts = lax.all_to_all(value.reshape(16, width // 16, -1), ("yl", "z", "yh"), 0, 0)
        return half(jnp.sum(parts.astype(F32), axis=0))

    def columns(value, name):
        spread = jnp.broadcast_to(value[None], (8, *value.shape))
        with jax.named_scope(name + "_columns"):
            parts = lax.all_to_all(spread, ("yh", "x"), 0, 0)
        return parts.reshape(2, 4, *value.shape)

    def rows_of(parts, x_index):
        return parts[:, x_index].reshape(-1, parts.shape[-1])

    def samples(value, name):
        with jax.named_scope(name + "_rows"):
            return lax.psum_scatter(value, SHARD, scatter_dimension=0, tiled=True)

    def halves(value, name, *others):
        with jax.named_scope(name + "_y"):
            came = after(across_y(value), *others) if others else across_y(value)
            return half(value.astype(F32) + came.astype(F32))

    sum_down, sum_gu = sum_cores(*grads_down), sum_cores(*grads_gu)
    rows_down = samples(sum_down, "down")
    d_attn = gather_x_async(after(half(keep * d_middle), rows_down), "d_attn_gather")
    unit_down = halves(rows_down, "down")
    ffn_branch = scatter_x(after(half(branch), d_attn), "branch_scatter")
    rows_gu = samples(after(sum_gu, d_attn, unit_down), "gate_up")
    output = both_cores(half(middle + keep * ffn_branch))

    d_heads = jnp.concatenate([half(mm(d_attn, part)) for part in packs_out], axis=1)
    d_query, key_part, value_part = attend_back(
        query, d_heads, heads_f, lse, all_keys, keys_t, all_values, key_tags, query_tags_t, cosine, sine
    )
    kv_part = after(jnp.concatenate([key_part, value_part], axis=1), ffn_branch)
    kv_mine = jnp.concatenate([kv_part[:count], kv_part[2 * count : 3 * count]], axis=0)
    kv_theirs = jnp.concatenate([kv_part[count : 2 * count], kv_part[3 * count :]], axis=0)
    kv_two = kv_mine + swap_cores(half(kv_theirs)).astype(F32)
    grad_kv = kv_two[:count] + across_y(half(kv_two[count:])).astype(F32)
    d_key = half(unrotate(grad_kv[:, :HD], cosine, sine))
    d_value = half(grad_kv[:, HD:])
    d_own = jnp.concatenate([d_query[:, :256], jnp.where(first, d_key, d_value)], axis=1)
    d_other = jnp.concatenate([d_query[:, 256:], jnp.where(first, d_value, d_key)], axis=1)
    d_normed_part = mm_nt(d_own, packs_qkv[0]) + mm_nt(d_other, packs_qkv[1])
    d_normed_attn = scatter_x_async(d_normed_part, "d_attn_scatter")
    input_part = norm_backward(xval, root_attn, gain_attn, d_normed_attn)
    input_grad = both_cores(half(d_middle + input_part))
    gain_attn_local = jnp.sum(d_normed_part * x_unit, axis=0)
    gains = half(jnp.stack([gain_attn_local, gain_ffn_local])).T
    sum_qkv = sum_cores(mm_tn(normed_attn, d_own), mm_tn(normed_attn, d_other))
    sum_out = sum_cores(mm_tn(d_attn, heads[:, :256]), mm_tn(d_attn, heads[:, 256:]))
    sums = jnp.concatenate([sum_qkv, sum_out], axis=1)
    sums = jnp.concatenate([sums, jnp.pad(gains, ((0, 0), (0, HD - 2)))], axis=1)
    total_rows = after(reduce_rows(sums, "attn"), rows_gu)
    packs = columns(total_rows, "attn")
    unit_rows = jnp.concatenate([halves(rows_gu, "gate_up", sum_qkv, sum_out), unit_down], axis=1)
    with jax.named_scope("unit_columns"):
        parts = lax.all_gather(unit_rows, "x", axis=0, tiled=False)
    grad_gate, grad_up, grad_down = spread(parts, tiles, spare)
    packs = after(packs.reshape(width // 2, -1), grad_gate).reshape(packs.shape)
    gains = jnp.sum(packs[..., 640:642].astype(F32), axis=1).reshape(-1, 2)
    gains = (gains + swap_cores(gains)).T
    packs = packs[..., :640]
    mine = lax.dynamic_slice_in_dim(packs, 2 * core, 2, axis=1)
    theirs = swap_cores(lax.dynamic_slice_in_dim(packs, 2 - 2 * core, 2, axis=1))
    grad_query, grad_key, grad_value, grad_out = place_heads(core, mine, theirs)
    return (
        output[None], input_grad[None], gains[0], gains[1],
        grad_query, grad_key, grad_value, grad_out, grad_gate, grad_up, grad_down,
    )


def solution(mesh):
    fine = Mesh(mesh.devices.reshape(2, 4, 2, 4, 2), ("yl", "z", "yh", "x", "tp"))
    shard, ctx = ("yl", "z"), ("yh", "x")
    acts, weight = P(shard, ctx, None), P(shard, "tp")
    return jax.shard_map(
        per_device,
        mesh=fine,
        in_specs=(acts, acts, P(shard, None), P(shard, None), P(shard), P(), P()) + (weight,) * 7,
        out_specs=(acts, acts, P(shard), P(shard)) + (weight,) * 7,
        check_vma=False,
    )
```

```python
import functools

import jax
import jax.numpy as jnp
from jax import lax
from jax.experimental import pallas as pl
from jax.experimental.pallas import tpu as pltpu
from jax.sharding import Mesh, PartitionSpec as P

HD = 128
EPS = 1e-05
NEG = -1e30
F32 = jnp.float32
BF16 = jnp.bfloat16
SHARD = ("yl", "z")
SCALE = HD ** (-0.5)
LOG2E = 1.4426950408889634
VMEM = 48 * 2**20
SWAP = ((0, 1), (1, 0))


def half(value):
    return value.astype(BF16)


def mm(left, right):
    return jnp.dot(left, right, preferred_element_type=F32)


def mm_nt(left, right):
    return lax.dot_general(left, right, (((1,), (1,)), ((), ())), preferred_element_type=F32)


def mm_tn(left, right):
    return lax.dot_general(left, right, (((0,), (0,)), ((), ())), preferred_element_type=F32)


def swap_cores(value, name="swap"):
    with jax.named_scope(name):
        return lax.ppermute(value, "tp", SWAP)


def across_y(value):
    return lax.ppermute(value, "yh", SWAP)


def after(value, *others):
    zero = sum((other[:1, :1] * 0).astype(value.dtype) for other in others)
    tile = value[:16, :HD] + zero
    return lax.dynamic_update_slice(value, tile, (0, 0))


def shift_x(value, hop):
    return lax.ppermute(value, "x", [(i, (i + hop) % 4) for i in range(4)])


def chunk(value, index):
    rows = value.shape[0] // 4
    return lax.dynamic_slice_in_dim(value, index % 4 * rows, rows, axis=0)


def gather_x(value, name):
    x_at = lax.axis_index("x")
    with jax.named_scope(name):
        moved = {hop: shift_x(value, -hop) for hop in (2, 1, 3)}
    chunks = [value, moved[1], moved[2], moved[3]]
    return [lax.select_n((i - x_at) % 4, *chunks) for i in range(4)]


def scatter_x(value, name):
    x_at = lax.axis_index("x")
    with jax.named_scope(name):
        moved = [shift_x(chunk(value, x_at + hop), hop) for hop in (2, 1, 3)]
    return sum((part.astype(F32) for part in moved), chunk(value, x_at).astype(F32))


def gather_x_async(value, name):
    with jax.named_scope(name):
        return lax.all_gather(value, "x", axis=0, tiled=True)


def scatter_x_async(value, name):
    with jax.named_scope(name):
        return lax.psum_scatter(half(value), "x", scatter_dimension=0, tiled=True).astype(F32)


def gather_shard(value):
    spread = jnp.broadcast_to(value[None], (8, *value.shape))
    return lax.all_to_all(spread, SHARD, 0, 0).reshape(-1, value.shape[1])


def rotate(value, cosine, sine):
    turned = jnp.concatenate([-value[..., HD // 2 :], value[..., : HD // 2]], axis=-1)
    return value * cosine + turned * sine


def unrotate(grad, cosine, sine):
    scaled = grad * sine
    return grad * cosine + jnp.concatenate(
        [scaled[..., HD // 2 :], -scaled[..., : HD // 2]], axis=-1
    )


def norm_root(value):
    return lax.rsqrt(jnp.mean(value * value, axis=-1, keepdims=True) + EPS)


def norm_backward(value, root, gain, grad):
    scaled = gain * grad
    return root * scaled - value * root**3 * jnp.mean(scaled * value, axis=-1, keepdims=True)


def attend_kernel(q_ref, kt_ref, v_ref, rows_ref, cols_ref, mixed_ref, heads_ref, lse_ref, bias_ref):
    @pl.when(pl.program_id(1) == 0)
    def _():
        seg, blk = rows_ref[:, :1], rows_ref[:, 1:2]
        visible = (seg == cols_ref[:1, :]) & (cols_ref[1:2, :] <= blk)
        bias_ref[...] = jnp.where(visible, 0.0, NEG)

    raw = mm(q_ref[...], kt_ref[...])
    raw = raw * (SCALE * LOG2E) + bias_ref[...]
    top = jnp.max(raw, axis=-1, keepdims=True)
    weights = jnp.exp2(raw - top)
    total = jnp.sum(weights, axis=-1, keepdims=True)
    mixed = mm(half(weights), v_ref[...]) / total
    mixed_ref[...] = mixed
    heads_ref[...] = half(mixed)
    lse = jnp.broadcast_to(top + jnp.log2(total), mixed.shape)
    lse_ref[0] = lse.T[:8, :]


def attend(query, keys_t, values, query_tags, key_tags_t, rows=256):
    count, features = query.shape
    n = values.shape[0]
    part = pl.BlockSpec((rows, HD), lambda j, h: (j, h))
    return pl.pallas_call(
        attend_kernel,
        grid=(count // rows, features // HD),
        in_specs=[
            part,
            pl.BlockSpec((HD, n), lambda j, h: (0, 0)),
            pl.BlockSpec((n, HD), lambda j, h: (0, 0)),
            pl.BlockSpec((rows, 2), lambda j, h: (j, 0)),
            pl.BlockSpec((2, n), lambda j, h: (0, 0)),
        ],
        out_specs=[part, part, pl.BlockSpec((1, 8, rows), lambda j, h: (h, 0, j))],
        out_shape=[
            jax.ShapeDtypeStruct((count, features), F32),
            jax.ShapeDtypeStruct((count, features), BF16),
            jax.ShapeDtypeStruct((features // HD, 8, count), F32),
        ],
        scratch_shapes=[pltpu.VMEM((rows, n), F32)],
        compiler_params=pltpu.CompilerParams(vmem_limit_bytes=VMEM),
        cost_estimate=pl.CostEstimate(
            flops=8 * count * features * n, transcendentals=count * features // HD * n, bytes_accessed=2**22
        ),
    )(query, keys_t, values, query_tags, key_tags_t)


def attend_back_kernel(
    q_ref, do_ref, mixed_ref, lse_ref, k_ref, kt_ref, v_ref, rows_ref, cols_ref, cos_ref, sin_ref,
    dq_ref, dk_ref, dv_ref, bias_ref, *, piece,
):
    @pl.when(pl.program_id(0) == 0)
    def _():
        dk_ref[...] = jnp.zeros_like(dk_ref)
        dv_ref[...] = jnp.zeros_like(dv_ref)
        seg, blk = rows_ref[:, :1], rows_ref[:, 1:2]
        visible = (seg == cols_ref[:1, :]) & (blk <= cols_ref[1:2, :])
        bias_ref[...] = jnp.where(visible, 0.0, NEG)

    q, d_out = q_ref[...], do_ref[...]
    wide = d_out.astype(F32)
    d_out_t = half(wide.T)
    qt = half(q.astype(F32).T)
    delta = jnp.sum((wide * mixed_ref[...]).T, axis=0, keepdims=True)
    lse = lse_ref[0, :1, :]
    grad_qt = jnp.zeros(qt.shape, F32)
    for at in range(0, k_ref.shape[0], piece):
        part = pl.ds(at, piece)
        raw = mm(k_ref[part, :], qt)
        probs = jnp.exp2(raw * (SCALE * LOG2E) + (bias_ref[part, :] - lse))
        d_probs = mm(v_ref[part, :], d_out_t)
        dv_ref[part, :] += mm(half(probs), d_out)
        d_scores = half(probs * (SCALE * (d_probs - delta)))
        dk_ref[part, :] += mm(d_scores, q)
        grad_qt += mm(kt_ref[:, part], d_scores)
    grad_q = grad_qt.T
    scaled = grad_q * sin_ref[...]
    lane = lax.broadcasted_iota(jnp.int32, scaled.shape, 1)
    turned = pltpu.roll(scaled, HD // 2, 1)
    dq_ref[...] = half(grad_q * cos_ref[...] + jnp.where(lane < HD // 2, turned, -turned))


def attend_back(query, d_heads, mixed, lse, keys, keys_t, values, key_tags, query_tags_t, cosine, sine):
    count, features = query.shape
    n = keys.shape[0]
    row = pl.BlockSpec((count, HD), lambda h: (0, h))

    def whole(*shape):
        return pl.BlockSpec(shape, lambda h: (0, 0))

    return pl.pallas_call(
        functools.partial(attend_back_kernel, piece=min(512, n)),
        grid=(features // HD,),
        in_specs=[
            row, row, row, pl.BlockSpec((1, 8, count), lambda h: (h, 0, 0)), whole(n, HD),
            whole(HD, n), whole(n, HD), whole(n, 2), whole(2, count), whole(count, HD), whole(count, HD),
        ],
        out_specs=[row, whole(n, HD), whole(n, HD)],
        out_shape=[
            jax.ShapeDtypeStruct((count, features), BF16),
            jax.ShapeDtypeStruct((n, HD), F32),
            jax.ShapeDtypeStruct((n, HD), F32),
        ],
        scratch_shapes=[pltpu.VMEM((n, count), F32)],
        compiler_params=pltpu.CompilerParams(vmem_limit_bytes=VMEM),
        cost_estimate=pl.CostEstimate(
            flops=20 * count * features * n, transcendentals=count * features // HD * n, bytes_accessed=2**23
        ),
    )(query, d_heads, mixed, lse, keys, keys_t, values, key_tags, query_tags_t, cosine, sine)


def place_heads_kernel(core_ref, mine_ref, theirs_ref, q_ref, k_ref, v_ref, o_ref):
    def place(first_ref, second_ref):
        for y in range(2):
            rows = pl.ds(y * first_ref.shape[2], first_ref.shape[2])
            for x in range(2):
                for i, ref in enumerate((first_ref, second_ref)):
                    lane = x * 512 + i * 256
                    q_ref[rows, lane : lane + 256] = ref[y, x, :, :256].astype(F32)
                    o_ref[rows, lane : lane + 256] = ref[y, x, :, 384:].astype(F32)
                k_ref[rows, x * HD : (x + 1) * HD] = first_ref[y, x, :, 256:384].astype(F32)
                v_ref[rows, x * HD : (x + 1) * HD] = second_ref[y, x, :, 256:384].astype(F32)

    @pl.when(core_ref[0] == 0)
    def _():
        place(mine_ref, theirs_ref)

    @pl.when(core_ref[0] != 0)
    def _():
        place(theirs_ref, mine_ref)


def place_heads(core, mine, theirs):
    rows = 2 * mine.shape[2]
    return pl.pallas_call(
        place_heads_kernel,
        in_specs=[
            pl.BlockSpec(memory_space=pltpu.SMEM),
            pl.BlockSpec(memory_space=pltpu.VMEM),
            pl.BlockSpec(memory_space=pltpu.VMEM),
        ],
        out_shape=[jax.ShapeDtypeStruct((rows, columns), F32) for columns in (1024, 256, 256, 1024)],
        compiler_params=pltpu.CompilerParams(vmem_limit_bytes=VMEM),
    )(core.reshape(1).astype(jnp.int32), mine, theirs)


def spread_kernel(parts_ref, *out_refs, tiles, spare):
    split = tiles + HD
    for place, out_ref in enumerate(out_refs):
        at = place * split
        for i in range(4):
            out_ref[:, i * tiles : (i + 1) * tiles] = parts_ref[i, :, at : at + tiles].astype(F32)
        rest = [parts_ref[i, :, at + tiles : at + split].astype(F32) for i in range(4)]
        for i in (0, 2):
            start = 4 * tiles + i * spare
            out_ref[:, start : start + HD] = rest[i] + pltpu.roll(rest[i + 1], spare, 1)


def spread(parts, tiles, spare, rows=64):
    _, count, columns = parts.shape
    outs = columns // (tiles + HD)
    units = 4 * (tiles + spare)
    return pl.pallas_call(
        functools.partial(spread_kernel, tiles=tiles, spare=spare),
        grid=(count // rows,),
        in_specs=[pl.BlockSpec((4, rows, columns), lambda j: (0, j, 0))],
        out_specs=[pl.BlockSpec((rows, units), lambda j: (j, 0))] * outs,
        out_shape=[jax.ShapeDtypeStruct((count, units), F32)] * outs,
        compiler_params=pltpu.CompilerParams(vmem_limit_bytes=VMEM),
    )(parts)


def per_device(
    tokens, cotangent, seq_ids, block_ids, keep_layer, gain_attn, gain_ffn,
    w_query, w_key, w_value, w_out, w_gate, w_up, w_down,
):
    core, x_at, y_at = lax.axis_index("tp"), lax.axis_index("x"), lax.axis_index("yh")
    first = core == 0
    rows = tokens.shape[1] // 2
    width = tokens.shape[2]
    keep = keep_layer[0].astype(F32)

    own_tokens = lax.dynamic_slice_in_dim(tokens[0], core * rows, rows, axis=0)
    own_top = lax.dynamic_slice_in_dim(cotangent[0], core * rows, rows, axis=0)
    x_top = gather_x_async(jnp.concatenate([own_tokens, own_top], axis=0), "token_gather")
    x_top = x_top.reshape(4, 2, rows, width)
    x_all, top_all = x_top[:, 0].reshape(-1, width), x_top[:, 1].reshape(-1, width)
    xval, grad_top = own_tokens.astype(F32), own_top.astype(F32)

    side = x_at // 2
    at = x_at % 2
    wq = half(lax.dynamic_slice_in_dim(w_query, at * 512, 512, axis=1))
    wk = half(lax.dynamic_slice_in_dim(w_key, at * HD, HD, axis=1))
    wv = half(lax.dynamic_slice_in_dim(w_value, at * HD, HD, axis=1))
    wo = half(lax.dynamic_slice_in_dim(w_out, at * 512, 512, axis=1))
    pack0 = jnp.concatenate([wq[:, :256], wk, wo[:, :256]], axis=1)
    pack1 = jnp.concatenate([wq[:, 256:], wv, wo[:, 256:]], axis=1)
    lent = lax.ppermute(
        jnp.where(first, pack1, pack0),
        ("x", "tp"),
        [(2 * i + i // 2, 2 * i + 1 - i // 2) for i in range(4)],
    )
    pack = jnp.where(core == side, jnp.where(first, pack0, pack1), lent)
    pack = gather_shard(pack)

    units = w_gate.shape[1] // 4
    tiles = units // HD * HD
    spare = units - tiles
    split = tiles + HD

    def hidden_units(weight):
        main = lax.dynamic_slice_in_dim(weight, x_at * tiles, tiles, axis=1)
        rest = lax.dynamic_slice_in_dim(weight[:, 4 * tiles :], x_at * spare, spare, axis=1)
        return jnp.concatenate([half(main), jnp.pad(half(rest), ((0, 0), (0, HD - spare)))], axis=1)

    own_ffn = jnp.concatenate([hidden_units(w) for w in (w_gate, w_up, w_down)], axis=1)
    with jax.named_scope("unit_gather"):
        own_ffn = lax.all_gather(after(own_ffn, pack), SHARD, axis=0, tiled=True)

    def of_positions(line, y_index, core_index):
        grid = line.reshape(2, 4, 2, rows)
        picked = lax.dynamic_index_in_dim(grid, y_index, 0, keepdims=False)
        picked = lax.dynamic_index_in_dim(picked, core_index, 1, keepdims=False)
        return picked.reshape(-1)

    corners = ((y_at, core), (y_at, 1 - core), (1 - y_at, core), (1 - y_at, 1 - core))
    lines = (seq_ids[0], block_ids[0])
    query_tags_t = jnp.stack([of_positions(line, y_at, core) for line in lines])
    key_tags_t = jnp.stack(
        [jnp.concatenate([of_positions(line, *corner) for corner in corners]) for line in lines]
    )
    query_tags, key_tags = query_tags_t.T, key_tags_t.T
    position = of_positions(jnp.arange(seq_ids.shape[1], dtype=jnp.int32), y_at, core)
    freqs = 10000.0 ** (-(jnp.arange(HD // 2).astype(F32) * 2.0 / HD))
    angle = position.astype(F32)[:, None] * freqs[None, :]
    cosine = jnp.concatenate([jnp.cos(angle), jnp.cos(angle)], axis=-1)
    sine = jnp.concatenate([jnp.sin(angle), jnp.sin(angle)], axis=-1)

    count = x_all.shape[0]
    x_all = x_all.astype(F32)
    x_unit = x_all * norm_root(x_all)
    normed_attn = half(x_unit * gain_attn)
    root_attn = norm_root(xval)
    packs_qkv = pack[:, :384], swap_cores(pack[:, :384])
    packs_out = pack[:, 384:], swap_cores(pack[:, 384:])
    own_pre, other_pre = [mm(normed_attn, part) for part in packs_qkv]
    key_pre = jnp.where(first, own_pre[:, 256:], other_pre[:, 256:])
    value_pre = jnp.where(first, other_pre[:, 256:], own_pre[:, 256:])
    query = jnp.concatenate(
        [half(rotate(pre[:, s : s + HD], cosine, sine)) for pre in (own_pre, other_pre) for s in (0, HD)],
        axis=1,
    )
    keys_values = jnp.concatenate([half(rotate(key_pre, cosine, sine)), half(value_pre)], axis=1)
    two_kv = jnp.concatenate([keys_values, across_y(keys_values)], axis=0)
    other_kv = swap_cores(two_kv)
    all_kv = jnp.concatenate(
        [two_kv[:count], other_kv[:count], two_kv[count:], other_kv[count:]], axis=0
    )
    all_keys, all_values = all_kv[:, :HD], all_kv[:, HD:]
    d_ffn = half(keep * top_all.astype(F32))

    keys_t = all_keys.T
    heads_f, heads, lse = attend(query, keys_t, all_values, query_tags, key_tags_t)

    attn_branch = mm_nt(heads[:, :256], packs_out[0]) + mm_nt(heads[:, 256:], packs_out[1])
    attn_branch = scatter_x(half(attn_branch), "attn_scatter")
    middle = xval + keep * attn_branch
    root_ffn = norm_root(middle)
    normed_ffn = jnp.concatenate(gather_x(half(middle * root_ffn * gain_ffn), "ffn_gather"), axis=0)

    own_ffn = after(own_ffn, normed_ffn)
    other_ffn = swap_cores(own_ffn)
    full_gu = (own_ffn[:, : 2 * split], other_ffn[:, : 2 * split])
    full_down = (own_ffn[:, 2 * split :], other_ffn[:, 2 * split :])
    branch = 0.0
    d_normed = 0.0
    d_gus, hiddens = [], []
    for wgu, wd in zip(full_gu, full_down, strict=True):
        gate_up = mm(after(normed_ffn, *hiddens[-1:]), wgu)
        gate, up = gate_up[:, :split], gate_up[:, split:]
        sig = jax.nn.sigmoid(gate)
        silu = gate * sig
        hidden = half(silu * up)
        d_hidden = mm(d_ffn, wd)
        d_gate = half(d_hidden * up * sig * (1.0 + gate * (1.0 - sig)))
        d_up = half(d_hidden * silu)
        d_gu = jnp.concatenate([d_gate, d_up], axis=1)
        d_normed = d_normed + mm_nt(d_gu, wgu)
        branch = branch + mm_nt(hidden, wd)
        d_gus.append(d_gu)
        hiddens.append(hidden)
    grads_down = [mm_tn(d_ffn, hidden) for hidden in hiddens]
    d_normed_ffn = scatter_x(half(d_normed), "d_ffn_scatter")
    left_gu = after(normed_ffn, d_normed_ffn)
    grads_gu = [mm_tn(left_gu, d_gu) for d_gu in d_gus]
    d_middle = grad_top + norm_backward(middle, root_ffn, gain_ffn, d_normed_ffn)
    gain_ffn_local = jnp.sum(d_normed_ffn * middle * root_ffn, axis=0)

    def both_cores(value):
        other = swap_cores(value)
        return jnp.concatenate(
            [jnp.where(first, value, other), jnp.where(first, other, value)], axis=0
        )

    def sum_cores(mine, theirs):
        return half(mine + swap_cores(half(theirs)).astype(F32))

    def reduce_rows(value, name):
        with jax.named_scope(name + "_rows"):
            parts = lax.all_to_all(value.reshape(16, value.shape[0] // 16, -1), ("yl", "z", "yh"), 0, 0)
        return half(jnp.sum(parts.astype(F32), axis=0))

    def columns(value, name):
        spread = jnp.broadcast_to(value[None], (8, *value.shape))
        with jax.named_scope(name + "_columns"):
            parts = lax.all_to_all(spread, ("yh", "x"), 0, 0)
        return parts.reshape(2, 4, *value.shape)

    def rows_of(parts, x_index):
        return parts[:, x_index].reshape(-1, parts.shape[-1])

    def samples(value, name):
        with jax.named_scope(name + "_rows"):
            return lax.psum_scatter(value, SHARD, scatter_dimension=0, tiled=True)

    def halves(value, name, *others):
        with jax.named_scope(name + "_y"):
            came = after(across_y(value), *others) if others else across_y(value)
            return half(value.astype(F32) + came.astype(F32))

    sum_down, sum_gu = sum_cores(*grads_down), sum_cores(*grads_gu)
    rows_down = samples(sum_down, "down")
    d_attn = gather_x_async(after(half(keep * d_middle), rows_down), "d_attn_gather")
    unit_down = halves(rows_down, "down")
    ffn_branch = scatter_x(after(half(branch), d_attn), "branch_scatter")
    rows_gu = samples(after(sum_gu, d_attn, unit_down), "gate_up")
    output = both_cores(half(middle + keep * ffn_branch))

    d_heads = jnp.concatenate([half(mm(d_attn, part)) for part in packs_out], axis=1)
    d_query, key_part, value_part = attend_back(
        query, d_heads, heads_f, lse, all_keys, keys_t, all_values, key_tags, query_tags_t, cosine, sine
    )
    kv_part = after(jnp.concatenate([key_part, value_part], axis=1), ffn_branch)
    kv_mine = jnp.concatenate([kv_part[:count], kv_part[2 * count : 3 * count]], axis=0)
    kv_theirs = jnp.concatenate([kv_part[count : 2 * count], kv_part[3 * count :]], axis=0)
    kv_two = kv_mine + swap_cores(half(kv_theirs)).astype(F32)
    grad_kv = kv_two[:count] + across_y(half(kv_two[count:])).astype(F32)
    d_key = half(unrotate(grad_kv[:, :HD], cosine, sine))
    d_value = half(grad_kv[:, HD:])
    d_own = jnp.concatenate([d_query[:, :256], jnp.where(first, d_key, d_value)], axis=1)
    d_other = jnp.concatenate([d_query[:, 256:], jnp.where(first, d_value, d_key)], axis=1)
    d_normed_part = mm_nt(d_own, packs_qkv[0]) + mm_nt(d_other, packs_qkv[1])
    d_normed_attn = scatter_x_async(d_normed_part, "d_attn_scatter")
    input_part = norm_backward(xval, root_attn, gain_attn, d_normed_attn)
    input_grad = both_cores(half(d_middle + input_part))
    gain_attn_local = jnp.sum(d_normed_part * x_unit, axis=0)
    gains = jnp.stack([half(gain_attn_local).reshape(16, -1), half(gain_ffn_local).reshape(16, -1)], axis=1)
    gains = gains.reshape(16, 1, width // 8)
    sum_qkv = sum_cores(mm_tn(normed_attn, d_own), mm_tn(normed_attn, d_other))
    sum_out = sum_cores(mm_tn(d_attn, heads[:, :256]), mm_tn(d_attn, heads[:, 256:]))
    sums = jnp.concatenate([sum_qkv, sum_out], axis=1)
    lines = jnp.pad(gains, ((0, 0), (0, 15), (0, sums.shape[1] - width // 8)))
    sums = jnp.concatenate([sums.reshape(16, width // 16, -1), lines], axis=1).reshape(-1, sums.shape[1])
    total_rows = after(reduce_rows(sums, "attn"), rows_gu)
    packs = columns(total_rows, "attn")
    unit_rows = jnp.concatenate([halves(rows_gu, "gate_up", sum_qkv, sum_out), unit_down], axis=1)
    with jax.named_scope("unit_columns"):
        parts = lax.all_gather(unit_rows, "x", axis=0, tiled=False)
    grad_gate, grad_up, grad_down = spread(parts, tiles, spare)
    packs = after(packs.reshape(-1, packs.shape[-1]), grad_gate).reshape(packs.shape)
    owned = width // 16
    gains = jnp.sum(packs[:, :, owned, : 2 * owned].astype(F32), axis=1)
    gains = (gains + swap_cores(gains)).reshape(2, 2, owned).transpose(1, 0, 2).reshape(2, -1)
    packs = packs[:, :, :owned]
    mine = lax.dynamic_slice_in_dim(packs, 2 * core, 2, axis=1)
    theirs = swap_cores(lax.dynamic_slice_in_dim(packs, 2 - 2 * core, 2, axis=1))
    grad_query, grad_key, grad_value, grad_out = place_heads(core, mine, theirs)
    return (
        output[None], input_grad[None], gains[0], gains[1],
        grad_query, grad_key, grad_value, grad_out, grad_gate, grad_up, grad_down,
    )


def solution(mesh):
    fine = Mesh(mesh.devices.reshape(2, 4, 2, 4, 2), ("yl", "z", "yh", "x", "tp"))
    shard, ctx = ("yl", "z"), ("yh", "x")
    acts, weight = P(shard, ctx, None), P(shard, "tp")
    return jax.shard_map(
        per_device,
        mesh=fine,
        in_specs=(acts, acts, P(shard, None), P(shard, None), P(shard), P(), P()) + (weight,) * 7,
        out_specs=(acts, acts, P(shard), P(shard)) + (weight,) * 7,
        check_vma=False,
    )
```
